32 devices in a mesh: grp: 2 (over x), row: 16 (over z, y, core).
Axes of the slice: x: 2, y: 2, z: 4, core: 2. Of those that a mesh axis runs over, the one named last changes fastest.
Arguments:
- coupling_features: bfloat16 [1024, 512, 128], P(('grp', 'row')), parts along dimension 0, may hold values from -6 to 6
- aligned_features: bfloat16 [256, 512, 256], P(('grp', 'row')), parts along dimension 0, may hold values from -6 to 6
- aligned_entry_flags: int32 [256, 512], P('grp'), parts along dimension 0, may hold values 0 or 1
- amino_real_flags: int32 [1024], P('grp'), parts along dimension 0, may hold values from 0 to 1, as said below
- coupling_offset_matrix: bfloat16 [128, 8], replicated, may hold values from -3.5 to 3.5
- lookup_matrices: bfloat16 [256, 1024], replicated, may hold values from -0.75 to 0.75
- aligned_final_matrix: bfloat16 [256, 256], replicated, may hold values from -0.375 to 0.375
- product_factor_matrices: bfloat16 [256, 64], replicated, may hold values from -0.375 to 0.375
- product_final_matrix: bfloat16 [1024, 128], replicated, may hold values from -1 to 1
- trio_factor_matrices: bfloat16 [128, 640], replicated, may hold values from -0.5 to 0.5
- trio_final_matrix: bfloat16 [128, 128], replicated, may hold values from -0.5 to 0.5
- feedforward_expand: bfloat16 [128, 512], replicated, may hold values from -0.5 to 0.5
- feedforward_shrink: bfloat16 [512, 128], replicated, may hold values from -0.25 to 0.25
Outputs:
- msa_out: bfloat16 [256, 512, 256], P(('grp', 'row')), parts along dimension 0
- coupling_refreshed: bfloat16 [1024, 512, 128], P(('grp', 'row')), parts along dimension 0
The draws below stay inside these ranges and needn't reach their ends.
There are 2 independent parts, one for each index of `grp`. The reference program is written for one: setup_inputs(seed, part) draws one part's arguments, and reference() takes and returns one part's arrays. A program takes and returns all parts, laid end to end along the dimension named above; an argument that names none is the same for every part. Nothing has to cross between parts.
Inputs may be any that keep to these rules, and one draw needn't show every extreme that they name: `amino_real_flags`: 1 on a prefix of at least 256 residues and 0 on the rest, which is never empty.
All inputs are finite; a program needn't handle non-finite values.
Results may differ from the reference program's by a relative error of at most 0.008.
The reference program's roundings to bfloat16 on the way count: a program that leaves them out, or rounds other values in their place, can miss the bound.
Values may be sent and summed in bfloat16 or wider, within the bound.
No kernel may reach another device: no remote copies, remote signals or barrier semaphores. Data moves between devices by JAX's collectives and lax.ppermute only.
A program may use at most 192 MiB of HBM per device.

```python
import jax
import jax.numpy as jnp
from jax import lax

CROP_RESIDUES = 512
ALIGNED_SEQS = 128
FEATURES_ALIGNED = 256
CZ = 128
HEADS = 8
HEAD_DIM = 32
C_OPM = 32
TRANS = 512


def draw_coupling_features(key, part):
    sample = jax.random.normal(key, (CROP_RESIDUES, CROP_RESIDUES, CZ), jnp.float32)
    return jnp.clip(sample, -6.0, 6.0).astype(jnp.bfloat16)


def draw_coupling_offset_matrix(key, part):
    return jax.random.uniform(key, (CZ, HEADS), jnp.float32, -0.3, 0.3).astype(jnp.bfloat16)


def draw_amino_real_flags(key, part):
    length = jax.random.randint(key, (), CROP_RESIDUES // 2, CROP_RESIDUES)
    return (jnp.arange(CROP_RESIDUES) < length).astype(jnp.int32)


def with_ends(array, rng, smallest, top_value):
    extent = array.shape
    index_at = [jax.random.randint(jax.random.fold_in(rng, axis), (), 0, extent[axis]) for axis in range(len(extent))]
    array = array.at[tuple(index_at)].set(smallest)
    longest = extent.index(max(extent))
    index_at[longest] = (index_at[longest] + 1) % extent[longest]
    return array.at[tuple(index_at)].set(top_value)


def block_levels(stream_key, extent, shards, smallest, top_value):
    loudness, own = 1.0, jax.random.fold_in(stream_key, 6)
    for position, blocks in shards:
        steps = jnp.exp(jax.random.uniform(jax.random.fold_in(own, position), (blocks,), jnp.float32, smallest / len(shards), top_value / len(shards)))
        loudness = loudness * jnp.repeat(steps, extent[position] // blocks).reshape([-1 if axis == position else 1 for axis in range(len(extent))])
    return loudness


def bell_draw(own_key, dims, scale, limit, cuts=(), kind=jnp.bfloat16):
    drawn = jax.random.normal(own_key, dims, jnp.float32) * scale
    if len(cuts) > 0:
        drawn = block_levels(own_key, dims, cuts, -0.22, 0.18) * drawn
    return jnp.clip(drawn, min=-limit, max=limit).astype(kind)


def setup_inputs(seed: int = 0, part: int = 0) -> dict:
    key_list = jax.random.split(jax.random.key(seed), 14)
    part_splits = jax.random.split(jax.random.fold_in(key_list[13], part), 14)
    return {
        "coupling_features": draw_coupling_features(jax.random.fold_in(jax.random.fold_in(key_list[13], part), 71), part),
        "aligned_features": bell_draw(part_splits[1], (ALIGNED_SEQS, CROP_RESIDUES, FEATURES_ALIGNED), 1.0, 6.0, ((0, 16),)),
        "aligned_entry_flags": with_ends((jax.random.randint(part_splits[2], (ALIGNED_SEQS, CROP_RESIDUES), 0, 5) < 4).astype(jnp.int32), jax.random.fold_in(part_splits[2], 1), 0, 1),
        "amino_real_flags": draw_amino_real_flags(jax.random.fold_in(jax.random.fold_in(key_list[13], part), 71), part),
        "coupling_offset_matrix": draw_coupling_offset_matrix(jax.random.fold_in(key_list[13], 71), part),
        "lookup_matrices": bell_draw(key_list[5], (FEATURES_ALIGNED, 4 * FEATURES_ALIGNED), (FEATURES_ALIGNED // 4) ** -0.5, 0.75),
        "aligned_final_matrix": bell_draw(key_list[6], (FEATURES_ALIGNED, FEATURES_ALIGNED), FEATURES_ALIGNED ** -0.5, 0.375),
        "product_factor_matrices": bell_draw(key_list[7], (FEATURES_ALIGNED, 2 * C_OPM), FEATURES_ALIGNED ** -0.5, 0.375),
        "product_final_matrix": bell_draw(key_list[8], (C_OPM * C_OPM, CZ), C_OPM ** -0.5, 1.0),
        "trio_factor_matrices": bell_draw(key_list[9], (CZ, 5 * CZ), CZ ** -0.5, 0.5),
        "trio_final_matrix": bell_draw(key_list[10], (CZ, CZ), CZ ** -0.5, 0.5),
        "feedforward_expand": bell_draw(key_list[11], (CZ, TRANS), CZ ** -0.5, 0.5),
        "feedforward_shrink": bell_draw(key_list[12], (TRANS, CZ), TRANS ** -0.5, 0.25),
    }


EPSILON = 1e-05

def standardize_features(values, dimension=-1):
    values = values.astype(jnp.float32)
    centered = values - lax.optimization_barrier(jnp.mean(values, axis=dimension, keepdims=True))
    variance = lax.optimization_barrier(jnp.mean(centered * centered, axis=dimension, keepdims=True))
    return centered * lax.rsqrt(variance + EPSILON)

def apply_matrix_map(values, weight):
    return jnp.einsum('...c,cd->...d', values.astype(jnp.float32), weight.astype(jnp.float32))

def reference(coupling_features, aligned_features, aligned_entry_flags, amino_real_flags, coupling_offset_matrix, lookup_matrices, aligned_final_matrix, product_factor_matrices, product_final_matrix, trio_factor_matrices, trio_final_matrix, feedforward_expand, feedforward_shrink):
    amino_real_valid = amino_real_flags.astype(jnp.float32)
    aligned_entry_valid = aligned_entry_flags.astype(jnp.float32) * amino_real_valid[None, :]
    pair_valid = amino_real_valid[:, None] * amino_real_valid[None, :]
    pair_normed = standardize_features(coupling_features).astype(jnp.bfloat16)
    bias_heads = jnp.einsum('ijc,ch->hij', pair_normed.astype(jnp.float32), coupling_offset_matrix.astype(jnp.float32)).astype(jnp.bfloat16)
    left_tri = (jax.nn.sigmoid(apply_matrix_map(pair_normed, trio_factor_matrices[:, 0:CZ])) * apply_matrix_map(pair_normed, trio_factor_matrices[:, CZ:2 * CZ]) * pair_valid[..., None]).astype(jnp.bfloat16)
    right_tri = (jax.nn.sigmoid(apply_matrix_map(pair_normed, trio_factor_matrices[:, 2 * CZ:3 * CZ])) * apply_matrix_map(pair_normed, trio_factor_matrices[:, 3 * CZ:4 * CZ]) * pair_valid[..., None]).astype(jnp.bfloat16)
    out_gate = jax.nn.sigmoid(apply_matrix_map(pair_normed, trio_factor_matrices[:, 4 * CZ:5 * CZ]))
    tri_sum = jnp.einsum('ikc,jkc->ijc', left_tri.astype(jnp.float32), right_tri.astype(jnp.float32)).astype(jnp.bfloat16)
    tri_normed = standardize_features(tri_sum).astype(jnp.bfloat16)
    pair_one = coupling_features.astype(jnp.float32) + out_gate * apply_matrix_map(tri_normed, trio_final_matrix)
    trans_hidden = jnp.maximum(apply_matrix_map(standardize_features(pair_one).astype(jnp.bfloat16), feedforward_expand), 0.0).astype(jnp.bfloat16)
    pair_two = pair_one + apply_matrix_map(trans_hidden, feedforward_shrink)
    aligned_standardized = standardize_features(aligned_features).astype(jnp.bfloat16)
    lookup_factors_all = apply_matrix_map(aligned_standardized, lookup_matrices)
    asking_vectors = (lookup_factors_all[..., 0:FEATURES_ALIGNED] * HEAD_DIM ** (-0.5)).astype(jnp.bfloat16).reshape(ALIGNED_SEQS, CROP_RESIDUES, HEADS, HEAD_DIM)
    lookup_subspaces = lookup_factors_all[..., FEATURES_ALIGNED:2 * FEATURES_ALIGNED].astype(jnp.bfloat16).reshape(ALIGNED_SEQS, CROP_RESIDUES, HEADS, HEAD_DIM)
    content_subspaces = lookup_factors_all[..., 2 * FEATURES_ALIGNED:3 * FEATURES_ALIGNED].astype(jnp.bfloat16).reshape(ALIGNED_SEQS, CROP_RESIDUES, HEADS, HEAD_DIM)
    aligned_sigmoid_factor = jax.nn.sigmoid(lookup_factors_all[..., 3 * FEATURES_ALIGNED:4 * FEATURES_ALIGNED])

    def softmax_mixing_for_one(operands):
        query_one, key_one, value_one, gate_one, valid_one = operands
        affinity_matrix = jnp.einsum('ihd,jhd->hij', query_one.astype(jnp.float32), key_one.astype(jnp.float32)) + bias_heads.astype(jnp.float32)
        affinity_matrix = jnp.where(valid_one[None, None, :] > 0, affinity_matrix, -1000000000.0)
        attn_weights = jax.nn.softmax(affinity_matrix, axis=-1).astype(jnp.bfloat16)
        combined_features = jnp.einsum('hij,jhd->ihd', attn_weights.astype(jnp.float32), value_one.astype(jnp.float32))
        return (combined_features.reshape(CROP_RESIDUES, FEATURES_ALIGNED) * gate_one).astype(jnp.bfloat16)
    softmax_mixed_result = lax.map(softmax_mixing_for_one, (asking_vectors, lookup_subspaces, content_subspaces, aligned_sigmoid_factor, aligned_entry_valid))
    aligned_refreshed = aligned_features.astype(jnp.float32) + apply_matrix_map(softmax_mixed_result, aligned_final_matrix)
    product_standardized = standardize_features(aligned_refreshed).astype(jnp.bfloat16)
    product_factors = apply_matrix_map(product_standardized, product_factor_matrices) * aligned_entry_valid[..., None]
    left_opm = product_factors[..., 0:C_OPM].astype(jnp.bfloat16)
    right_opm = product_factors[..., C_OPM:2 * C_OPM].astype(jnp.bfloat16)
    coupling_tally = jnp.dot(aligned_entry_valid.T, aligned_entry_valid, precision=lax.Precision.HIGHEST)

    def outer_rows(block_index):
        first_row = (block_index * 32).astype(jnp.int32)
        left_part = lax.dynamic_slice_in_dim(left_opm, first_row, 32, 1)
        raw_outer = jnp.einsum('sic,sjd->ijcd', left_part.astype(jnp.float32), right_opm.astype(jnp.float32)).astype(jnp.bfloat16)
        return apply_matrix_map(raw_outer.reshape(32, CROP_RESIDUES, C_OPM * C_OPM), product_final_matrix)
    opm_sum = lax.map(outer_rows, jnp.arange(CROP_RESIDUES // 32, dtype=jnp.int32)).reshape(CROP_RESIDUES, CROP_RESIDUES, CZ)
    coupling_refreshed = (pair_two + opm_sum / jnp.maximum(coupling_tally, 1.0)[..., None]).astype(jnp.bfloat16)
    return (aligned_refreshed.astype(jnp.bfloat16), coupling_refreshed)
```

```python
import functools

import jax
import jax.numpy as jnp
from jax import lax
from jax.experimental import pallas as pl
from jax.experimental.pallas import tpu as pltpu
from jax.sharding import PartitionSpec as P


EPSILON = 1e-05
F32 = jnp.float32
BF16 = jnp.bfloat16
LANES = 128
HEAD_UNROLL = 4
TAIL_UNROLL = 4


def norm(values, axis=-1):
    centered = values - jnp.mean(values, axis=axis, keepdims=True)
    variance = jnp.mean(centered * centered, axis=axis, keepdims=True)
    return centered * lax.rsqrt(variance + EPSILON)


def dot(a, b, ca=1, cb=0):
    return lax.dot_general(a, b, (((ca,), (cb,)), ((), ())), preferred_element_type=F32)


def divisor(total, limit):
    best = min(total, limit)
    while total % best:
        best -= 1
    return best


def put_rows(scr, first, rows, values):
    for n in range(scr.shape[0]):
        scr[n, pl.ds(first, values.shape[0], stride=rows), :] = values[:, n * LANES : (n + 1) * LANES]


def get_rows(scr, first, rows):
    count = scr.shape[1] // rows
    return jnp.concatenate([scr[n, pl.ds(first, count, stride=rows), :] for n in range(scr.shape[0])], axis=1)


def full(shape):
    return pl.BlockSpec(shape, lambda *_: (0,) * len(shape))


def head_kernel(rows, with_bias, x_ref, vi_ref, vj_ref, w_ref, *refs):
    if with_bias:
        wb_ref, tri_ref, bias_ref, scr = refs
    else:
        tri_ref, scr = refs
    cz = x_ref.shape[2]
    heads = wb_ref.shape[0] if with_bias else 0

    def row(i, carry):
        xn = norm(x_ref[i].astype(F32)).astype(BF16)
        both = dot(w_ref[...], xn, 1, 1)
        valid = vj_ref[...] * vi_ref[0, i]
        put_rows(scr, i, rows, jax.nn.sigmoid(both[0:cz]) * both[cz : 2 * cz] * valid)
        if with_bias:
            put_rows(scr, cz * rows + i, rows, dot(wb_ref[...], xn, 1, 1))
        return carry

    lax.fori_loop(0, rows, row, 0, unroll=HEAD_UNROLL)
    for n in range(scr.shape[0]):
        cols = slice(n * LANES, (n + 1) * LANES)
        tri_ref[:, :, cols] = scr[n, 0 : cz * rows].astype(BF16).reshape(cz, rows, LANES)
        if with_bias:
            bias_ref[:, :, cols] = scr[n, cz * rows :].astype(BF16).reshape(heads, rows, LANES)


def pair_head(x, my_valid, valid, w, wb=None, part=0, parts=1):
    owned, res, cz = x.shape
    owned = owned // parts
    rows = divisor(owned, 16)
    steps = owned // rows
    heads = 0 if wb is None else wb.shape[0]
    in_specs = [
        pl.BlockSpec((rows, res, cz), lambda g: (g + part * steps, 0, 0)),
        pl.BlockSpec((1, 1, rows), lambda g: (g + part * steps, 0, 0), memory_space=pltpu.SMEM),
        full((1, res)),
        full(w.shape),
    ]
    args = [x, my_valid.reshape(-1, 1, rows), valid.reshape(1, res), w]
    out_specs = [pl.BlockSpec((cz, rows, res), lambda g: (0, g, 0))]
    out_shape = [jax.ShapeDtypeStruct((cz, owned, res), BF16)]
    if heads:
        in_specs.append(full(wb.shape))
        args.append(wb)
        out_specs.append(pl.BlockSpec((heads, rows, res), lambda g: (0, g, 0)))
        out_shape.append(jax.ShapeDtypeStruct((heads, owned, res), BF16))

    def kernel(x_ref, vi_ref, vj_ref, w_ref, *refs):
        head_kernel(rows, heads > 0, x_ref, vi_ref.at[0], vj_ref, w_ref, *refs)

    return pl.pallas_call(
        kernel,
        grid=(steps,),
        in_specs=in_specs,
        out_specs=out_specs,
        out_shape=out_shape,
        scratch_shapes=[pltpu.VMEM((res // LANES, (cz + heads) * rows, LANES), F32)],
        name="pair_head_bias" if heads else "pair_head",
    )(*args)


def msa_kernel(width, chunk, x_ref, valid_ref, bias_ref, w_ref, wf_ref, wp_ref, o_ref, l_ref, r_ref, q_s, k_s, v_s, att):
    res, feat = x_ref.shape[1:]
    half = feat // 2
    per_half = half // width
    x = x_ref[0].astype(F32)
    xn = norm(x).astype(BF16)
    q_s[...] = (dot(xn, w_ref[:, 0:feat]) * width ** (-0.5)).astype(BF16)
    k_s[...] = dot(xn, w_ref[:, feat : 2 * feat]).astype(BF16)
    v_s[...] = dot(xn, w_ref[:, 2 * feat : 3 * feat]).astype(BF16)
    valid = valid_ref[0]
    lane = lax.broadcasted_iota(jnp.int32, (1, feat), 1) // width
    lane_half = lax.broadcasted_iota(jnp.int32, (1, half), 1) // width

    def heads(step, carry):
        for side in (0, 1):
            mine = lane == step + side * per_half
            mine_half = lane_half == step
            v = jnp.where(mine, v_s[...], jnp.ones((), BF16))
            for c in range(res // chunk):
                span = slice(c * chunk, (c + 1) * chunk)
                q = jnp.where(mine, q_s[span], jnp.zeros((), BF16))
                s = dot(q, k_s[...], 1, 1) + bias_ref[step + side * per_half, span].astype(F32)
                s = jnp.where(valid > 0, s, -1000000000.0)
                p = jnp.exp(s - jnp.max(s, axis=1, keepdims=True)).astype(BF16)
                out = dot(p, v)
                mixed = out[:, side * half : (side + 1) * half] / out[:, (1 - side) * half : (2 - side) * half]
                cols = slice(side * half, (side + 1) * half)
                att[span, cols] = jnp.where(mine_half, mixed, att[span, cols])
        return carry

    lax.fori_loop(0, per_half, heads, 0)
    gate = jax.nn.sigmoid(dot(xn, w_ref[:, 3 * feat : 4 * feat]))
    mixed = (att[...] * gate).astype(BF16)
    new = x + dot(mixed, wf_ref[...])
    o_ref[0] = new.astype(BF16)
    factors = dot(wp_ref[...], norm(new).astype(BF16), 1, 1) * valid
    outer = l_ref.shape[1]
    l_ref[0] = factors[0:outer].astype(BF16)
    r_ref[0] = factors[outer : 2 * outer].astype(BF16)


def msa_block(x, valid, bias, w, wf, wp, width):
    seqs, res, feat = x.shape
    outer = wp.shape[0] // 2
    return pl.pallas_call(
        functools.partial(msa_kernel, width, divisor(res, 256)),
        grid=(seqs,),
        in_specs=[
            pl.BlockSpec((1, res, feat), lambda s: (s, 0, 0)),
            pl.BlockSpec((1, 1, res), lambda s: (s, 0, 0)),
            full(bias.shape),
            full(w.shape),
            full(wf.shape),
            full(wp.shape),
        ],
        out_specs=[
            pl.BlockSpec((1, res, feat), lambda s: (s, 0, 0)),
            pl.BlockSpec((1, outer, res), lambda s: (s, 0, 0)),
            pl.BlockSpec((1, outer, res), lambda s: (s, 0, 0)),
        ],
        out_shape=[
            jax.ShapeDtypeStruct((seqs, res, feat), BF16),
            jax.ShapeDtypeStruct((seqs, outer, res), BF16),
            jax.ShapeDtypeStruct((seqs, outer, res), BF16),
        ],
        scratch_shapes=[pltpu.VMEM((res, feat), BF16)] * 3 + [pltpu.VMEM((res, feat), F32)],
        name="msa_block",
    )(x, valid.reshape(seqs, 1, res), bias, w, wf, wp)


def tri_kernel(l_ref, *refs):
    groups, chans, owned, res = l_ref.shape
    o_ref = refs[-1]
    for c in range(chans):
        a = l_ref[:, c].reshape(groups * owned, res)
        for n, r_ref in enumerate(refs[:-1]):
            count = groups * r_ref.shape[2]
            part = dot(a, r_ref[:, c].reshape(count, res), 1, 1).astype(BF16)
            o_ref[:, c, :, n * count : (n + 1) * count] = part.reshape(groups, owned, count)


def tri_sums(left, rights):
    groups, chans, owned, res = left.shape
    step = divisor(chans, 4)

    def spec(rows, cols):
        return pl.BlockSpec((groups, step, rows, cols), lambda c: (0, c, 0, 0))

    cols = groups * sum(r.shape[2] for r in rights)
    return pl.pallas_call(
        tri_kernel,
        grid=(chans // step,),
        in_specs=[spec(owned, res)] + [spec(r.shape[2], res) for r in rights],
        out_specs=spec(owned, cols),
        out_shape=jax.ShapeDtypeStruct((groups, chans, owned, cols), BF16),
        name="tri_sums",
    )(left, *rights)


def opm_kernel(l_ref, r_ref, w_ref, vt_ref, vi_ref, o_ref, mix):
    rows, seqs, outer = l_ref.shape
    cz = o_ref.shape[2]
    inner = w_ref.shape[1] // cz
    for first in range(0, rows, 2):
        pair = min(2, rows - first)
        both = l_ref[first : first + pair].reshape(pair * seqs, outer)
        for d in range(inner):
            part = dot(both, w_ref[:, d * cz : (d + 1) * cz]).astype(BF16)
            for n in range(pair):
                mix[d * seqs : (d + 1) * seqs, n * cz : (n + 1) * cz] = part[n * seqs : (n + 1) * seqs]
        total = dot(r_ref[...], mix[:, 0 : pair * cz])
        for n in range(pair):
            mine = jnp.broadcast_to(vi_ref[:, first + n : first + n + 1], (seqs, cz)).astype(BF16)
            tally = jnp.maximum(dot(vt_ref[...], mine), 1.0)
            o_ref[first + n] = total[:, n * cz : (n + 1) * cz] / tally


def opm_block(left, right, w, valid_t, mine):
    owned, seqs, outer = left.shape
    res, depth = right.shape
    cz = w.shape[1] // (depth // seqs)
    rows = divisor(owned, 8)
    return pl.pallas_call(
        opm_kernel,
        grid=(owned // rows,),
        in_specs=[
            pl.BlockSpec((rows, seqs, outer), lambda g: (g, 0, 0)),
            full(right.shape),
            full(w.shape),
            full(valid_t.shape),
            pl.BlockSpec((None, seqs, rows), lambda g: (g, 0, 0)),
        ],
        out_specs=pl.BlockSpec((rows, res, cz), lambda g: (g, 0, 0)),
        out_shape=jax.ShapeDtypeStruct((owned, res, cz), F32),
        scratch_shapes=[pltpu.VMEM((depth, 2 * cz), BF16)],
        name="opm_block",
    )(left, right, w, valid_t, mine.reshape(seqs, owned // rows, rows).transpose(1, 0, 2))


def tail_kernel(half_ref, x_ref, tri_ref, opm_ref, wg_ref, wt_ref, w1_ref, w2_ref, *refs):
    o_ref, scr = refs[-2:]
    rows, groups, lines, cz = x_ref.shape
    for n in range(scr.shape[0]):
        part = tri_ref[:, :, n * LANES : (n + 1) * LANES]
        scr[n] = part.astype(F32).reshape(scr.shape[1:])

    def row(i, carry):
        x = x_ref[i].reshape(groups * lines, cz).astype(F32)
        gate = jax.nn.sigmoid(dot(norm(x).astype(BF16), wg_ref[...]))
        tri = norm(get_rows(scr, i, rows), 0).astype(BF16)
        one = x + gate * dot(tri, wt_ref[...], 0, 0)
        hidden = jnp.maximum(dot(norm(one).astype(BF16), w1_ref[...]), 0.0).astype(BF16)
        out = one + dot(hidden, w2_ref[...]) + opm_ref[i].reshape(groups * lines, cz)
        o_ref[i] = out.astype(BF16).reshape(groups, lines, cz)
        return carry

    lax.fori_loop(0, rows, row, 0, unroll=TAIL_UNROLL)


def pair_tail(half, first, parts, x, tri, opm, wg, wt, w1, w2, earlier=None):
    owned, res, cz = x.shape
    ring = res // owned
    rows = divisor(owned, 16)
    lines = owned // parts
    span = ring // 2 * lines
    count = tri.shape[2] // span
    view = (owned, ring, parts, lines, cz)
    pair = pl.BlockSpec((rows, ring // 2, None, lines, cz), lambda q, g, h: (g, h[0], first + q, 0, 0))
    in_specs = [
        pair,
        pl.BlockSpec((cz, rows, span), lambda q, g, h: (0, g, q)),
        pair,
        full(wg.shape),
        full(wt.shape),
        full(w1.shape),
        full(w2.shape),
    ]
    args = [half, x.reshape(view), tri, opm.reshape(view), wg, wt, w1, w2]
    if earlier is not None:
        in_specs.append(pl.BlockSpec(memory_space=pl.ANY))
        args.append(earlier.reshape(view))
    return pl.pallas_call(
        tail_kernel,
        grid_spec=pltpu.PrefetchScalarGridSpec(
            num_scalar_prefetch=1,
            grid=(count, owned // rows),
            in_specs=in_specs,
            out_specs=pair,
            scratch_shapes=[pltpu.VMEM((max(span // LANES, 1), cz * rows, min(span, LANES)), F32)],
        ),
        out_shape=jax.ShapeDtypeStruct(view, BF16),
        input_output_aliases={} if earlier is None else {8: 0},
        name="pair_tail",
    )(*args).reshape(owned, res, cz)


def body(
    ring,
    coupling_features,
    aligned_features,
    aligned_entry_flags,
    amino_real_flags,
    coupling_offset_matrix,
    lookup_matrices,
    aligned_final_matrix,
    product_factor_matrices,
    product_final_matrix,
    trio_factor_matrices,
    trio_final_matrix,
    feedforward_expand,
    feedforward_shrink,
):
    owned, res, cz = coupling_features.shape
    seqs, _, feat = aligned_features.shape
    width = feat // coupling_offset_matrix.shape[1]
    outer = product_factor_matrices.shape[1] // 2
    place = lax.axis_index("row")
    near = ring // 2
    halves = [list(range(near)), list(range(near, ring))]
    swap = [(r, (r + near) % ring) for r in range(ring)]

    residue = amino_real_flags.astype(F32)
    entry = aligned_entry_flags.astype(F32) * residue[None, :]
    my_residue = lax.dynamic_slice_in_dim(residue, place * owned, owned, 0)
    my_entry = lax.dynamic_slice_in_dim(entry, place * seqs, seqs, 0)
    trio = trio_factor_matrices.T

    parts = 2 if owned % 32 == 0 else 1
    half = (place // near).astype(jnp.int32).reshape(1)

    def spread(values):
        values = values.reshape(near, cz // near, values.shape[1], values.shape[-1])
        return lax.all_to_all(values, "row", 0, 0, tiled=True, axis_index_groups=halves)

    made = [
        pair_head(coupling_features, my_residue, residue, trio[2 * cz : 4 * cz], coupling_offset_matrix.T, part, parts)
        for part in range(parts)
    ]
    bias = jnp.concatenate([b for _, b in made], axis=1)
    right_own, right_oth = [], []
    for part in range(parts):
        right_own.append(spread(made[part][0]))
        right_oth.append(lax.ppermute(right_own[part], "row", swap))
    (left,) = pair_head(coupling_features, my_residue, residue, trio[0 : 2 * cz])
    left_own = spread(left)
    bias_all = lax.all_gather(bias, "row", axis=1, tiled=True)

    msa_out, left_opm, right_opm = msa_block(
        aligned_features,
        my_entry,
        bias_all,
        lookup_matrices,
        aligned_final_matrix,
        product_factor_matrices.T,
        width,
    )

    def collect(sums):
        back = lax.all_to_all(sums, "row", 0, 0, tiled=True, axis_index_groups=halves)
        return back.reshape(cz, owned, sums.shape[-1])

    sums = tri_sums(left_own, right_own)
    tri_own = collect(sums)
    tri_oth = []
    for part in range(parts):
        sums = tri_sums(left_own, [right_oth[part]])
        tri_oth.append(collect(sums))

    left_res = lax.all_to_all(left_opm, "row", split_axis=2, concat_axis=0, tiled=True).transpose(2, 0, 1)
    right_all = lax.all_gather(right_opm.transpose(1, 0, 2), "row", axis=1, tiled=True)
    right_all = right_all.reshape(outer * ring * seqs, res).T
    mine = lax.dynamic_slice_in_dim(entry, place * owned, owned, 1)
    opm = opm_block(left_res, right_all, product_final_matrix.reshape(outer, outer * cz), entry.T.astype(BF16), mine)
    weights = (trio_factor_matrices[:, 4 * cz : 5 * cz], trio_final_matrix, feedforward_expand, feedforward_shrink)
    pair = pair_tail(half, 0, parts, coupling_features, tri_own, opm, *weights)
    for part in range(parts):
        pair = pair_tail(1 - half, part, parts, coupling_features, tri_oth[part], opm, *weights, earlier=pair)
    return (msa_out, pair)


def solution(mesh):
    return jax.shard_map(
        functools.partial(body, mesh.shape["row"]),
        mesh=mesh,
        in_specs=(
            P(("grp", "row"), None, None),
            P(("grp", "row"), None, None),
            P("grp", None),
            P("grp"),
            P(),
            P(),
            P(),
            P(),
            P(),
            P(),
            P(),
            P(),
            P(),
        ),
        out_specs=(P(("grp", "row"), None, None), P(("grp", "row"), None, None)),
        check_vma=False,
    )
```

```python
import functools

import jax
import jax.numpy as jnp
from jax import lax
from jax.experimental import pallas as pl
from jax.experimental.pallas import tpu as pltpu
from jax.sharding import PartitionSpec as P


EPSILON = 1e-05
F32 = jnp.float32
BF16 = jnp.bfloat16
LANES = 128
HEAD_UNROLL = 4
TAIL_UNROLL = 2
TAIL_ROWS = 8


def norm(values, axis=-1):
    centered = values - jnp.mean(values, axis=axis, keepdims=True)
    variance = jnp.mean(centered * centered, axis=axis, keepdims=True)
    return centered * lax.rsqrt(variance + EPSILON)


def dot(a, b, ca=1, cb=0):
    return lax.dot_general(a, b, (((ca,), (cb,)), ((), ())), preferred_element_type=F32)


def divisor(total, limit):
    best = min(total, limit)
    while total % best:
        best -= 1
    return best


def put_rows(scr, first, rows, values):
    for n in range(scr.shape[0]):
        scr[n, pl.ds(first, values.shape[0], stride=rows), :] = values[:, n * LANES : (n + 1) * LANES]


def get_rows(scr, first, rows):
    count = scr.shape[1] // rows
    return jnp.concatenate([scr[n, pl.ds(first, count, stride=rows), :] for n in range(scr.shape[0])], axis=1)


def full(shape):
    return pl.BlockSpec(shape, lambda *_: (0,) * len(shape))


def head_kernel(rows, with_bias, x_ref, vi_ref, vj_ref, w_ref, *refs):
    if with_bias:
        wb_ref, tri_ref, bias_ref, scr = refs
    else:
        tri_ref, scr = refs
    cz = x_ref.shape[2]
    heads = wb_ref.shape[0] if with_bias else 0

    def row(i, carry):
        xn = norm(x_ref[i].astype(F32)).astype(BF16)
        both = dot(w_ref[...], xn, 1, 1)
        valid = vj_ref[...] * vi_ref[0, i]
        put_rows(scr, i, rows, jax.nn.sigmoid(both[0:cz]) * both[cz : 2 * cz] * valid)
        if with_bias:
            put_rows(scr, cz * rows + i, rows, dot(wb_ref[...], xn, 1, 1))
        return carry

    lax.fori_loop(0, rows, row, 0, unroll=HEAD_UNROLL)
    for n in range(scr.shape[0]):
        cols = slice(n * LANES, (n + 1) * LANES)
        tri_ref[:, :, cols] = scr[n, 0 : cz * rows].astype(BF16).reshape(cz, rows, LANES)
        if with_bias:
            bias_ref[:, :, cols] = scr[n, cz * rows :].astype(BF16).reshape(heads, rows, LANES)


def pair_head(x, my_valid, valid, w, wb=None, part=0, parts=1):
    owned, res, cz = x.shape
    owned = owned // parts
    rows = divisor(owned, 16)
    steps = owned // rows
    heads = 0 if wb is None else wb.shape[0]
    in_specs = [
        pl.BlockSpec((rows, res, cz), lambda g: (g + part * steps, 0, 0)),
        pl.BlockSpec((1, 1, rows), lambda g: (g + part * steps, 0, 0), memory_space=pltpu.SMEM),
        full((1, res)),
        full(w.shape),
    ]
    args = [x, my_valid.reshape(-1, 1, rows), valid.reshape(1, res), w]
    out_specs = [pl.BlockSpec((cz, rows, res), lambda g: (0, g, 0))]
    out_shape = [jax.ShapeDtypeStruct((cz, owned, res), BF16)]
    if heads:
        in_specs.append(full(wb.shape))
        args.append(wb)
        out_specs.append(pl.BlockSpec((heads, rows, res), lambda g: (0, g, 0)))
        out_shape.append(jax.ShapeDtypeStruct((heads, owned, res), BF16))

    def kernel(x_ref, vi_ref, vj_ref, w_ref, *refs):
        head_kernel(rows, heads > 0, x_ref, vi_ref.at[0], vj_ref, w_ref, *refs)

    return pl.pallas_call(
        kernel,
        grid=(steps,),
        in_specs=in_specs,
        out_specs=out_specs,
        out_shape=out_shape,
        scratch_shapes=[pltpu.VMEM((res // LANES, (cz + heads) * rows, LANES), F32)],
        name="pair_head_bias" if heads else "pair_head",
    )(*args)


def msa_kernel(width, chunk, order, x_ref, valid_ref, bias_ref, w_ref, wf_ref, wp_ref, o_ref, l_ref, r_ref, q_s, k_s, v_s, att):
    res, feat = x_ref.shape[1:]
    half = feat // 2
    per_half = half // width
    x = x_ref[0].astype(F32)
    xn = norm(x).astype(BF16)
    q_s[...] = (dot(xn, w_ref[:, 0:feat]) * width ** (-0.5)).astype(BF16)
    k_s[...] = dot(xn, w_ref[:, feat : 2 * feat]).astype(BF16)
    v_s[...] = dot(xn, w_ref[:, 2 * feat : 3 * feat]).astype(BF16)
    valid = valid_ref[0]
    lane = lax.broadcasted_iota(jnp.int32, (1, feat), 1) // width
    lane_half = lax.broadcasted_iota(jnp.int32, (1, half), 1) // width

    def heads(step, carry):
        for side in (0, 1):
            mine = lane == step + side * per_half
            mine_half = lane_half == step
            v = jnp.where(mine, v_s[...], jnp.ones((), BF16))
            for c in range(res // chunk):
                span = slice(c * chunk, (c + 1) * chunk)
                q = jnp.where(mine, q_s[span], jnp.zeros((), BF16))
                lines = bias_ref.shape[2]
                owners = order[c * chunk // lines : (c + 1) * chunk // lines]
                bias = jnp.concatenate([bias_ref[g, step + side * per_half] for g in owners], axis=0)
                s = dot(q, k_s[...], 1, 1) + bias.astype(F32)
                s = jnp.where(valid > 0, s, -1000000000.0)
                p = jnp.exp(s - jnp.max(s, axis=1, keepdims=True)).astype(BF16)
                out = dot(p, v)
                mixed = out[:, side * half : (side + 1) * half] / out[:, (1 - side) * half : (2 - side) * half]
                cols = slice(side * half, (side + 1) * half)
                att[span, cols] = jnp.where(mine_half, mixed, att[span, cols])
        return carry

    lax.fori_loop(0, per_half, heads, 0)
    gate = jax.nn.sigmoid(dot(xn, w_ref[:, 3 * feat : 4 * feat]))
    mixed = (att[...] * gate).astype(BF16)
    new = x + dot(mixed, wf_ref[...])
    o_ref[0] = new.astype(BF16)
    factors = dot(wp_ref[...], norm(new).astype(BF16), 1, 1) * valid
    outer = l_ref.shape[1]
    l_ref[0] = factors[0:outer].astype(BF16)
    r_ref[0] = factors[outer : 2 * outer].astype(BF16)


def msa_block(x, valid, bias, order, w, wf, wp, width):
    seqs, res, feat = x.shape
    outer = wp.shape[0] // 2
    return pl.pallas_call(
        functools.partial(msa_kernel, width, divisor(res, 256), order),
        grid=(seqs,),
        in_specs=[
            pl.BlockSpec((1, res, feat), lambda s: (s, 0, 0)),
            pl.BlockSpec((1, 1, res), lambda s: (s, 0, 0)),
            full(bias.shape),
            full(w.shape),
            full(wf.shape),
            full(wp.shape),
        ],
        out_specs=[
            pl.BlockSpec((1, res, feat), lambda s: (s, 0, 0)),
            pl.BlockSpec((1, outer, res), lambda s: (s, 0, 0)),
            pl.BlockSpec((1, outer, res), lambda s: (s, 0, 0)),
        ],
        out_shape=[
            jax.ShapeDtypeStruct((seqs, res, feat), BF16),
            jax.ShapeDtypeStruct((seqs, outer, res), BF16),
            jax.ShapeDtypeStruct((seqs, outer, res), BF16),
        ],
        scratch_shapes=[pltpu.VMEM((res, feat), BF16)] * 3 + [pltpu.VMEM((res, feat), F32)],
        name="msa_block",
    )(x, valid.reshape(seqs, 1, res), bias, w, wf, wp)


def tri_kernel(l_ref, *refs):
    groups, chans, owned, res = l_ref.shape
    o_ref = refs[-1]
    for c in range(chans):
        a = l_ref[:, c].reshape(groups * owned, res)
        for n, r_ref in enumerate(refs[:-1]):
            count = groups * r_ref.shape[2]
            part = dot(a, r_ref[:, c].reshape(count, res), 1, 1).astype(BF16)
            o_ref[:, c, :, n * count : (n + 1) * count] = part.reshape(groups, owned, count)


def tri_sums(left, rights):
    groups, chans, owned, res = left.shape
    step = divisor(chans, 4)

    def spec(rows, cols):
        return pl.BlockSpec((groups, step, rows, cols), lambda c: (0, c, 0, 0))

    cols = groups * sum(r.shape[2] for r in rights)
    return pl.pallas_call(
        tri_kernel,
        grid=(chans // step,),
        in_specs=[spec(owned, res)] + [spec(r.shape[2], res) for r in rights],
        out_specs=spec(owned, cols),
        out_shape=jax.ShapeDtypeStruct((groups, chans, owned, cols), BF16),
        name="tri_sums",
    )(left, *rights)


def opm_kernel(l_ref, r_ref, w_ref, vt_ref, vi_ref, two_ref, o_ref, sum_ref, mix, right):
    rows, seqs, outer = l_ref.shape
    owners, inner, local, res = r_ref.shape
    cz = o_ref.shape[2]
    depth = inner * local

    @pl.when(pl.program_id(0) == 0)
    def _():
        for g in range(owners):
            right[:, g * depth : (g + 1) * depth] = r_ref[g].reshape(depth, res).T

    many = max(16 // local, 1)
    for first in range(0, rows, 2):
        pair = min(2, rows - first)
        both = l_ref[first : first + pair].reshape(pair * seqs, outer)
        for d in range(0, inner, many):
            made = [dot(both, w_ref[:, (d + m) * cz : (d + m + 1) * cz]) for m in range(many)]
            for n in range(pair):
                for g in range(owners):
                    at = n * seqs + g * local
                    lines = jnp.concatenate([t[at : at + local] for t in made], axis=0).astype(BF16)
                    to = g * depth + d * local
                    mix[to : to + many * local, n * cz : (n + 1) * cz] = lines
        total = dot(right[...], mix[:, 0 : pair * cz])
        for n in range(pair):
            mine = jnp.broadcast_to(vi_ref[:, first + n : first + n + 1], (seqs, cz)).astype(BF16)
            tally = jnp.maximum(dot(vt_ref[...], mine), 1.0)
            mean = total[:, n * cz : (n + 1) * cz] / tally
            o_ref[first + n] = mean
            sum_ref[first + n] = (mean + two_ref[first + n]).astype(BF16)


def opm_block(left, right, w, valid_t, mine, two):
    owned, seqs, outer = left.shape
    _, inner, _, res = right.shape
    cz = w.shape[1] // inner
    rows = divisor(owned, 8)
    pair = pl.BlockSpec((rows, res, cz), lambda g: (g, 0, 0))
    return pl.pallas_call(
        opm_kernel,
        grid=(owned // rows,),
        in_specs=[
            pl.BlockSpec((rows, seqs, outer), lambda g: (g, 0, 0)),
            full(right.shape),
            full(w.shape),
            full(valid_t.shape),
            pl.BlockSpec((None, seqs, rows), lambda g: (g, 0, 0)),
            pair,
        ],
        out_specs=[pair, pair],
        out_shape=[
            jax.ShapeDtypeStruct((owned, res, cz), F32),
            jax.ShapeDtypeStruct((owned, res, cz), BF16),
        ],
        scratch_shapes=[pltpu.VMEM((seqs * inner, 2 * cz), BF16), pltpu.VMEM((res, seqs * inner), BF16)],
        name="opm_block",
    )(left, right, w, valid_t, mine.reshape(seqs, owned // rows, rows).transpose(1, 0, 2), two)


def tail_kernel(last, half_ref, x_ref, tri_ref, wg_ref, wt_ref, w1_ref, w2_ref, *refs):
    opm_ref = refs[0]
    o_ref, scr = refs[-2:]
    rows, groups, lines, cz = x_ref.shape
    cols = groups * lines
    many = divisor(rows, TAIL_ROWS)
    for n in range(scr.shape[0]):
        part = tri_ref[:, :, n * LANES : (n + 1) * LANES]
        scr[n] = part.astype(F32).reshape(scr.shape[1:])

    def block(b, carry):
        i = b * many
        x = x_ref[pl.ds(i, many)].reshape(many * cols, cz).astype(F32)
        gate = jax.nn.sigmoid(dot(norm(x).astype(BF16), wg_ref[...]))
        tri = [dot(norm(get_rows(scr, i + m, rows), 0).astype(BF16), wt_ref[...], 0, 0) for m in range(many)]
        one = x + gate * jnp.concatenate(tri, axis=0)
        hidden = jnp.maximum(dot(norm(one).astype(BF16), w1_ref[...]), 0.0).astype(BF16)
        out = one + dot(hidden, w2_ref[...])
        if last:
            out = out + opm_ref[pl.ds(i, many)].reshape(many * cols, cz)
        o_ref[pl.ds(i, many)] = out.astype(o_ref.dtype).reshape(many, groups, lines, cz)
        return carry

    lax.fori_loop(0, rows // many, block, 0, unroll=TAIL_UNROLL)


def pair_tail(half, first, parts, x, tri, weights, opm=None, earlier=None):
    owned, res, cz = x.shape
    ring = res // owned
    rows = divisor(owned, 16)
    lines = owned // parts
    span = ring // 2 * lines
    count = tri.shape[2] // span
    last = opm is not None
    view = (owned, ring, parts, lines, cz)
    pair = pl.BlockSpec((rows, ring // 2, None, lines, cz), lambda q, g, h: (g, h[0], first + q, 0, 0))
    in_specs = [pair, pl.BlockSpec((cz, rows, span), lambda q, g, h: (0, g, q))] + [full(w.shape) for w in weights]
    args = [half, x.reshape(view), tri, *weights]
    if last:
        in_specs.append(pair)
        args.append(opm.reshape(view))
    aliases = {}
    if earlier is not None:
        aliases = {len(args): 0}
        in_specs.append(pl.BlockSpec(memory_space=pl.ANY))
        args.append(earlier.reshape(view))
    return pl.pallas_call(
        functools.partial(tail_kernel, last),
        grid_spec=pltpu.PrefetchScalarGridSpec(
            num_scalar_prefetch=1,
            grid=(count, owned // rows),
            in_specs=in_specs,
            out_specs=pair,
            scratch_shapes=[pltpu.VMEM((max(span // LANES, 1), cz * rows, min(span, LANES)), F32)],
        ),
        out_shape=jax.ShapeDtypeStruct(view, BF16 if last else F32),
        input_output_aliases=aliases,
        name="pair_tail_last" if last else "pair_tail",
    )(*args).reshape(owned, res, cz)


def body(
    ring,
    coupling_features,
    aligned_features,
    aligned_entry_flags,
    amino_real_flags,
    coupling_offset_matrix,
    lookup_matrices,
    aligned_final_matrix,
    product_factor_matrices,
    product_final_matrix,
    trio_factor_matrices,
    trio_final_matrix,
    feedforward_expand,
    feedforward_shrink,
):
    owned, res, cz = coupling_features.shape
    seqs, _, feat = aligned_features.shape
    width = feat // coupling_offset_matrix.shape[1]
    outer = product_factor_matrices.shape[1] // 2
    place = lax.axis_index("row")
    near = ring // 2
    halves = [list(range(near)), list(range(near, ring))]
    swap = [(r, (r + near) % ring) for r in range(ring)]

    residue = amino_real_flags.astype(F32)
    entry = aligned_entry_flags.astype(F32) * residue[None, :]
    my_residue = lax.dynamic_slice_in_dim(residue, place * owned, owned, 0)
    my_entry = lax.dynamic_slice_in_dim(entry, place * seqs, seqs, 0)
    trio = trio_factor_matrices.T

    parts = 2 if owned % 32 == 0 else 1
    half = (place // near).astype(jnp.int32).reshape(1)

    def spread(values):
        values = values.reshape(near, cz // near, values.shape[1], values.shape[-1])
        return lax.all_to_all(values, "row", 0, 0, tiled=True, axis_index_groups=halves)

    made = [
        pair_head(coupling_features, my_residue, residue, trio[2 * cz : 4 * cz], coupling_offset_matrix.T, part, parts)
        for part in range(parts)
    ]
    bias = jnp.concatenate([b for _, b in made], axis=1)
    right_own, right_oth = [], []
    for part in range(parts):
        right_own.append(spread(made[part][0]))
        right_oth.append(lax.ppermute(right_own[part], "row", swap))
    (left,) = pair_head(coupling_features, my_residue, residue, trio[0 : 2 * cz])
    left_own = spread(left)
    planes = 4 if ring % 4 == 0 else 1
    members = ring // planes
    across = [[m + members * z for z in range(planes)] for m in range(members)]
    within = [[m + members * z for m in range(members)] for z in range(planes)]
    order = [m * planes + z for z in range(planes) for m in range(members)]

    def gather(values):
        values = lax.all_gather(values, "row", axis=0, axis_index_groups=across)
        values = lax.all_gather(values, "row", axis=0, axis_index_groups=within)
        return values.reshape((ring,) + values.shape[2:])

    bias_all = gather(bias)

    msa_out, left_opm, right_opm = msa_block(
        aligned_features,
        my_entry,
        bias_all,
        order,
        lookup_matrices,
        aligned_final_matrix,
        product_factor_matrices.T,
        width,
    )

    def collect(sums):
        back = lax.all_to_all(sums, "row", 0, 0, tiled=True, axis_index_groups=halves)
        return back.reshape(cz, owned, sums.shape[-1])

    sums = tri_sums(left_own, right_own)
    tri_own = collect(sums)
    tri_oth = []
    for part in range(parts):
        sums = tri_sums(left_own, [right_oth[part]])
        tri_oth.append(collect(sums))

    right_all = gather(right_opm.transpose(1, 0, 2))
    left_res = lax.all_to_all(left_opm, "row", split_axis=2, concat_axis=0, tiled=True).transpose(2, 0, 1)
    left_res = left_res.reshape(owned, planes, members, seqs, outer).transpose(0, 2, 1, 3, 4)
    left_res = left_res.reshape(owned, ring * seqs, outer)
    entry_order = entry.reshape(planes, members, seqs, res).transpose(1, 0, 2, 3).reshape(ring * seqs, res)
    mine = lax.dynamic_slice_in_dim(entry_order, place * owned, owned, 1)
    weights = (trio_factor_matrices[:, 4 * cz : 5 * cz], trio_final_matrix, feedforward_expand, feedforward_shrink)
    two = pair_tail(half, 0, parts, coupling_features, tri_own, weights)
    for part in range(parts - 1):
        two = pair_tail(1 - half, part, parts, coupling_features, tri_oth[part], weights, earlier=two)
    opm, pair = opm_block(
        left_res,
        right_all,
        product_final_matrix.reshape(outer, outer * cz),
        entry_order.T.astype(BF16),
        mine,
        two,
    )
    pair = pair_tail(
        1 - half, parts - 1, parts, coupling_features, tri_oth[-1], weights, opm=opm, earlier=pair
    )
    return (msa_out, pair)


def solution(mesh):
    return jax.shard_map(
        functools.partial(body, mesh.shape["row"]),
        mesh=mesh,
        in_specs=(
            P(("grp", "row"), None, None),
            P(("grp", "row"), None, None),
            P("grp", None),
            P("grp"),
            P(),
            P(),
            P(),
            P(),
            P(),
            P(),
            P(),
            P(),
            P(),
        ),
        out_specs=(P(("grp", "row"), None, None), P(("grp", "row"), None, None)),
        check_vma=False,
    )
```

```python
import functools

import jax
import jax.numpy as jnp
from jax import lax
from jax.experimental import pallas as pl
from jax.experimental.pallas import tpu as pltpu
from jax.sharding import PartitionSpec as P


EPSILON = 1e-05
F32 = jnp.float32
BF16 = jnp.bfloat16
LANES = 128
HEAD_UNROLL = 4
TAIL_UNROLL = 2
TAIL_ROWS = 8


def norm(values, axis=-1):
    centered = values - jnp.mean(values, axis=axis, keepdims=True)
    variance = jnp.mean(centered * centered, axis=axis, keepdims=True)
    return centered * lax.rsqrt(variance + EPSILON)


def dot(a, b, ca=1, cb=0):
    return lax.dot_general(a, b, (((ca,), (cb,)), ((), ())), preferred_element_type=F32)


def divisor(total, limit):
    best = min(total, limit)
    while total % best:
        best -= 1
    return best


def put_rows(scr, first, rows, values):
    for n in range(scr.shape[0]):
        scr[n, pl.ds(first, values.shape[0], stride=rows), :] = values[:, n * LANES : (n + 1) * LANES]


def get_rows(scr, first, rows):
    count = scr.shape[1] // rows
    return jnp.concatenate([scr[n, pl.ds(first, count, stride=rows), :] for n in range(scr.shape[0])], axis=1)


def full(shape):
    return pl.BlockSpec(shape, lambda *_: (0,) * len(shape))


def head_kernel(rows, with_bias, x_ref, vi_ref, vj_ref, w_ref, *refs):
    if with_bias:
        wb_ref, tri_ref, bias_ref, scr = refs
    else:
        tri_ref, scr = refs
    cz = x_ref.shape[2]
    heads = wb_ref.shape[0] if with_bias else 0

    def row(i, carry):
        xn = norm(x_ref[i].astype(F32)).astype(BF16)
        both = dot(w_ref[...], xn, 1, 1)
        valid = vj_ref[...] * vi_ref[0, i]
        put_rows(scr, i, rows, jax.nn.sigmoid(both[0:cz]) * both[cz : 2 * cz] * valid)
        if with_bias:
            put_rows(scr, cz * rows + i, rows, dot(wb_ref[...], xn, 1, 1))
        return carry

    lax.fori_loop(0, rows, row, 0, unroll=HEAD_UNROLL)
    for n in range(scr.shape[0]):
        cols = slice(n * LANES, (n + 1) * LANES)
        tri_ref[:, :, cols] = scr[n, 0 : cz * rows].astype(BF16).reshape(cz, rows, LANES)
        if with_bias:
            bias_ref[:, :, cols] = scr[n, cz * rows :].astype(BF16).reshape(heads, rows, LANES)


def pair_head(x, my_valid, valid, w, wb=None, part=0, parts=1):
    owned, res, cz = x.shape
    owned = owned // parts
    rows = divisor(owned, 16)
    steps = owned // rows
    heads = 0 if wb is None else wb.shape[0]
    in_specs = [
        pl.BlockSpec((rows, res, cz), lambda g: (g + part * steps, 0, 0)),
        pl.BlockSpec((1, 1, rows), lambda g: (g + part * steps, 0, 0), memory_space=pltpu.SMEM),
        full((1, res)),
        full(w.shape),
    ]
    args = [x, my_valid.reshape(-1, 1, rows), valid.reshape(1, res), w]
    out_specs = [pl.BlockSpec((cz, rows, res), lambda g: (0, g, 0))]
    out_shape = [jax.ShapeDtypeStruct((cz, owned, res), BF16)]
    if heads:
        in_specs.append(full(wb.shape))
        args.append(wb)
        out_specs.append(pl.BlockSpec((heads, rows, res), lambda g: (0, g, 0)))
        out_shape.append(jax.ShapeDtypeStruct((heads, owned, res), BF16))

    def kernel(x_ref, vi_ref, vj_ref, w_ref, *refs):
        head_kernel(rows, heads > 0, x_ref, vi_ref.at[0], vj_ref, w_ref, *refs)

    return pl.pallas_call(
        kernel,
        grid=(steps,),
        in_specs=in_specs,
        out_specs=out_specs,
        out_shape=out_shape,
        scratch_shapes=[pltpu.VMEM((res // LANES, (cz + heads) * rows, LANES), F32)],
        name="pair_head_bias" if heads else "pair_head",
    )(*args)


def msa_kernel(width, chunk, order, x_ref, valid_ref, bias_ref, w_ref, wf_ref, wp_ref, o_ref, l_ref, r_ref, q_s, k_s, v_s, att):
    res, feat = x_ref.shape[1:]
    half = feat // 2
    per_half = half // width
    x = x_ref[0].astype(F32)
    xn = norm(x).astype(BF16)
    q_s[...] = (dot(xn, w_ref[:, 0:feat]) * width ** (-0.5)).astype(BF16)
    k_s[...] = dot(xn, w_ref[:, feat : 2 * feat]).astype(BF16)
    v_s[...] = dot(xn, w_ref[:, 2 * feat : 3 * feat]).astype(BF16)
    valid = valid_ref[0]
    lane = lax.broadcasted_iota(jnp.int32, (1, feat), 1) // width
    lane_half = lax.broadcasted_iota(jnp.int32, (1, half), 1) // width

    def heads(step, carry):
        for side in (0, 1):
            mine = lane == step + side * per_half
            mine_half = lane_half == step
            v = jnp.where(mine, v_s[...], jnp.ones((), BF16))
            for c in range(res // chunk):
                span = slice(c * chunk, (c + 1) * chunk)
                q = jnp.where(mine, q_s[span], jnp.zeros((), BF16))
                lines = bias_ref.shape[2]
                owners = order[c * chunk // lines : (c + 1) * chunk // lines]
                bias = jnp.concatenate([bias_ref[g, step + side * per_half] for g in owners], axis=0)
                s = dot(q, k_s[...], 1, 1) + bias.astype(F32)
                s = jnp.where(valid > 0, s, -1000000000.0)
                p = jnp.exp(s - jnp.max(s, axis=1, keepdims=True)).astype(BF16)
                out = dot(p, v)
                mixed = out[:, side * half : (side + 1) * half] / out[:, (1 - side) * half : (2 - side) * half]
                cols = slice(side * half, (side + 1) * half)
                att[span, cols] = jnp.where(mine_half, mixed, att[span, cols])
        return carry

    lax.fori_loop(0, per_half, heads, 0)
    gate = jax.nn.sigmoid(dot(xn, w_ref[:, 3 * feat : 4 * feat]))
    mixed = (att[...] * gate).astype(BF16)
    new = x + dot(mixed, wf_ref[...])
    o_ref[0] = new.astype(BF16)
    factors = dot(wp_ref[...], norm(new).astype(BF16), 1, 1) * valid
    outer = l_ref.shape[1]
    l_ref[0] = factors[0:outer].astype(BF16)
    r_ref[0] = factors[outer : 2 * outer].astype(BF16)


def msa_block(x, valid, bias, order, w, wf, wp, width):
    seqs, res, feat = x.shape
    outer = wp.shape[0] // 2
    return pl.pallas_call(
        functools.partial(msa_kernel, width, divisor(res, 256), order),
        grid=(seqs,),
        in_specs=[
            pl.BlockSpec((1, res, feat), lambda s: (s, 0, 0)),
            pl.BlockSpec((1, 1, res), lambda s: (s, 0, 0)),
            full(bias.shape),
            full(w.shape),
            full(wf.shape),
            full(wp.shape),
        ],
        out_specs=[
            pl.BlockSpec((1, res, feat), lambda s: (s, 0, 0)),
            pl.BlockSpec((1, outer, res), lambda s: (s, 0, 0)),
            pl.BlockSpec((1, outer, res), lambda s: (s, 0, 0)),
        ],
        out_shape=[
            jax.ShapeDtypeStruct((seqs, res, feat), BF16),
            jax.ShapeDtypeStruct((seqs, outer, res), BF16),
            jax.ShapeDtypeStruct((seqs, outer, res), BF16),
        ],
        scratch_shapes=[pltpu.VMEM((res, feat), BF16)] * 3 + [pltpu.VMEM((res, feat), F32)],
        name="msa_block",
    )(x, valid.reshape(seqs, 1, res), bias, w, wf, wp)


def tri_kernel(l_ref, *refs):
    groups, chans, owned, res = l_ref.shape
    o_ref = refs[-1]
    for c in range(chans):
        a = l_ref[:, c].reshape(groups * owned, res)
        for n, r_ref in enumerate(refs[:-1]):
            count = groups * r_ref.shape[2]
            part = dot(a, r_ref[:, c].reshape(count, res), 1, 1).astype(BF16)
            o_ref[:, c, :, n * count : (n + 1) * count] = part.reshape(groups, owned, count)


def tri_sums(left, rights):
    groups, chans, owned, res = left.shape
    step = divisor(chans, 4)

    def spec(rows, cols):
        return pl.BlockSpec((groups, step, rows, cols), lambda c: (0, c, 0, 0))

    cols = groups * sum(r.shape[2] for r in rights)
    return pl.pallas_call(
        tri_kernel,
        grid=(chans // step,),
        in_specs=[spec(owned, res)] + [spec(r.shape[2], res) for r in rights],
        out_specs=spec(owned, cols),
        out_shape=jax.ShapeDtypeStruct((groups, chans, owned, cols), BF16),
        name="tri_sums",
    )(left, *rights)


def opm_kernel(l_ref, r_ref, w_ref, vt_ref, vi_ref, two_ref, o_ref, sum_ref, mix, right):
    rows, seqs, outer = l_ref.shape
    owners, inner, local, res = r_ref.shape
    cz = o_ref.shape[2]
    depth = inner * local

    @pl.when(pl.program_id(0) == 0)
    def _():
        for g in range(owners):
            right[:, g * depth : (g + 1) * depth] = r_ref[g].reshape(depth, res).T

    many = max(16 // local, 1)
    for first in range(0, rows, 2):
        pair = min(2, rows - first)
        both = l_ref[first : first + pair].reshape(pair * seqs, outer)
        for d in range(0, inner, many):
            made = [dot(both, w_ref[:, (d + m) * cz : (d + m + 1) * cz]) for m in range(many)]
            for n in range(pair):
                for g in range(owners):
                    at = n * seqs + g * local
                    lines = jnp.concatenate([t[at : at + local] for t in made], axis=0).astype(BF16)
                    to = g * depth + d * local
                    mix[to : to + many * local, n * cz : (n + 1) * cz] = lines
        total = dot(right[...], mix[:, 0 : pair * cz])
        for n in range(pair):
            mine = jnp.broadcast_to(vi_ref[:, first + n : first + n + 1], (seqs, cz)).astype(BF16)
            tally = jnp.maximum(dot(vt_ref[...], mine), 1.0)
            mean = total[:, n * cz : (n + 1) * cz] / tally
            o_ref[first + n] = mean
            sum_ref[first + n] = (mean + two_ref[first + n]).astype(BF16)


def opm_block(left, right, w, valid_t, mine, two):
    owned, seqs, outer = left.shape
    _, inner, _, res = right.shape
    cz = w.shape[1] // inner
    rows = divisor(owned, 8)
    pair = pl.BlockSpec((rows, res, cz), lambda g: (g, 0, 0))
    return pl.pallas_call(
        opm_kernel,
        grid=(owned // rows,),
        in_specs=[
            pl.BlockSpec((rows, seqs, outer), lambda g: (g, 0, 0)),
            full(right.shape),
            full(w.shape),
            full(valid_t.shape),
            pl.BlockSpec((None, seqs, rows), lambda g: (g, 0, 0)),
            pair,
        ],
        out_specs=[pair, pair],
        out_shape=[
            jax.ShapeDtypeStruct((owned, res, cz), F32),
            jax.ShapeDtypeStruct((owned, res, cz), BF16),
        ],
        scratch_shapes=[pltpu.VMEM((seqs * inner, 2 * cz), BF16), pltpu.VMEM((res, seqs * inner), BF16)],
        name="opm_block",
    )(left, right, w, valid_t, mine.reshape(seqs, owned // rows, rows).transpose(1, 0, 2), two)


def tail_kernel(last, half_ref, x_ref, tri_ref, wg_ref, wt_ref, w1_ref, w2_ref, *refs):
    opm_ref = refs[0]
    o_ref, scr = refs[-2:]
    rows, groups, lines, cz = x_ref.shape
    cols = groups * lines
    many = divisor(rows, TAIL_ROWS)
    for n in range(scr.shape[0]):
        part = tri_ref[:, :, n * LANES : (n + 1) * LANES]
        scr[n] = part.astype(F32).reshape(scr.shape[1:])

    def block(b, carry):
        i = b * many
        x = x_ref[pl.ds(i, many)].reshape(many * cols, cz).astype(F32)
        gate = jax.nn.sigmoid(dot(norm(x).astype(BF16), wg_ref[...]))
        tri = [dot(norm(get_rows(scr, i + m, rows), 0).astype(BF16), wt_ref[...], 0, 0) for m in range(many)]
        one = x + gate * jnp.concatenate(tri, axis=0)
        hidden = jnp.maximum(dot(norm(one).astype(BF16), w1_ref[...]), 0.0).astype(BF16)
        out = one + dot(hidden, w2_ref[...])
        if last:
            out = out + opm_ref[pl.ds(i, many)].reshape(many * cols, cz)
        o_ref[pl.ds(i, many)] = out.astype(o_ref.dtype).reshape(many, groups, lines, cz)
        return carry

    lax.fori_loop(0, rows // many, block, 0, unroll=TAIL_UNROLL)


def pair_tail(half, first, parts, x, tri, weights, opm=None, earlier=None):
    owned, res, cz = x.shape
    ring = res // owned
    rows = divisor(owned, 16)
    lines = owned // parts
    span = ring // 2 * lines
    count = tri.shape[2] // span
    last = opm is not None
    view = (owned, ring, parts, lines, cz)
    pair = pl.BlockSpec((rows, ring // 2, None, lines, cz), lambda q, g, h: (g, h[0], first + q, 0, 0))
    in_specs = [pair, pl.BlockSpec((cz, rows, span), lambda q, g, h: (0, g, q))] + [full(w.shape) for w in weights]
    args = [half, x.reshape(view), tri, *weights]
    if last:
        in_specs.append(pair)
        args.append(opm.reshape(view))
    aliases = {}
    if earlier is not None:
        aliases = {len(args): 0}
        in_specs.append(pl.BlockSpec(memory_space=pl.ANY))
        args.append(earlier.reshape(view))
    return pl.pallas_call(
        functools.partial(tail_kernel, last),
        grid_spec=pltpu.PrefetchScalarGridSpec(
            num_scalar_prefetch=1,
            grid=(count, owned // rows),
            in_specs=in_specs,
            out_specs=pair,
            scratch_shapes=[pltpu.VMEM((max(span // LANES, 1), cz * rows, min(span, LANES)), F32)],
        ),
        out_shape=jax.ShapeDtypeStruct(view, BF16 if last else F32),
        input_output_aliases=aliases,
        name="pair_tail_last" if last else "pair_tail",
    )(*args).reshape(owned, res, cz)


def body(
    ring,
    coupling_features,
    aligned_features,
    aligned_entry_flags,
    amino_real_flags,
    coupling_offset_matrix,
    lookup_matrices,
    aligned_final_matrix,
    product_factor_matrices,
    product_final_matrix,
    trio_factor_matrices,
    trio_final_matrix,
    feedforward_expand,
    feedforward_shrink,
):
    owned, res, cz = coupling_features.shape
    seqs, _, feat = aligned_features.shape
    width = feat // coupling_offset_matrix.shape[1]
    outer = product_factor_matrices.shape[1] // 2
    place = lax.axis_index("row")
    near = ring // 2
    halves = [list(range(near)), list(range(near, ring))]
    swap = [(r, (r + near) % ring) for r in range(ring)]

    residue = amino_real_flags.astype(F32)
    entry = aligned_entry_flags.astype(F32) * residue[None, :]
    my_residue = lax.dynamic_slice_in_dim(residue, place * owned, owned, 0)
    my_entry = lax.dynamic_slice_in_dim(entry, place * seqs, seqs, 0)
    trio = trio_factor_matrices.T

    parts = 2 if owned % 32 == 0 else 1
    half = (place // near).astype(jnp.int32).reshape(1)

    def spread(values):
        values = values.reshape(near, cz // near, values.shape[1], values.shape[-1])
        return lax.all_to_all(values, "row", 0, 0, tiled=True, axis_index_groups=halves)

    made = [
        pair_head(coupling_features, my_residue, residue, trio[2 * cz : 4 * cz], coupling_offset_matrix.T, part, parts)
        for part in range(parts)
    ]
    bias = jnp.concatenate([b for _, b in made], axis=1)

    planes = 4 if ring % 4 == 0 else 1
    members = ring // planes
    plane = place // members
    within = [[m + members * z for m in range(members)] for z in range(planes)]
    order = [m * planes + z for z in range(planes) for m in range(members)]

    def across(values):
        got = [values]
        for k in range(1, planes):
            got.append(lax.ppermute(values, "row", [(r, r ^ (k * members)) for r in range(ring)]))
        got = jnp.stack(got)
        return jnp.stack([lax.dynamic_index_in_dim(got, plane ^ z, 0, keepdims=False) for z in range(planes)])

    def gather(values):
        values = lax.all_gather(values, "row", axis=0, axis_index_groups=within)
        return values.reshape((ring,) + values.shape[2:])

    bias = across(bias)
    right_own, right_oth = [], []
    for part in range(parts):
        right = made[part][0]
        if part:
            right, bias = lax.optimization_barrier((right, bias))
        right_own.append(spread(right))
        right_oth.append(lax.ppermute(right_own[part], "row", swap))
    (left,) = pair_head(coupling_features, my_residue, residue, trio[0 : 2 * cz])
    left_own = spread(left)
    bias_all = gather(bias)

    msa_out, left_opm, right_opm = msa_block(
        aligned_features,
        my_entry,
        bias_all,
        order,
        lookup_matrices,
        aligned_final_matrix,
        product_factor_matrices.T,
        width,
    )

    def collect(sums):
        back = lax.all_to_all(sums, "row", 0, 0, tiled=True, axis_index_groups=halves)
        return back.reshape(cz, owned, sums.shape[-1])

    sums = tri_sums(left_own, right_own)
    tri_own = collect(sums)
    tri_oth = []
    for part in range(parts):
        sums = tri_sums(left_own, [right_oth[part]])
        tri_oth.append(collect(sums))

    right_all = gather(across(right_opm.transpose(1, 0, 2)))
    left_res = lax.all_to_all(left_opm, "row", split_axis=2, concat_axis=0, tiled=True).transpose(2, 0, 1)
    left_res = left_res.reshape(owned, planes, members, seqs, outer).transpose(0, 2, 1, 3, 4)
    left_res = left_res.reshape(owned, ring * seqs, outer)
    entry_order = entry.reshape(planes, members, seqs, res).transpose(1, 0, 2, 3).reshape(ring * seqs, res)
    mine = lax.dynamic_slice_in_dim(entry_order, place * owned, owned, 1)
    weights = (trio_factor_matrices[:, 4 * cz : 5 * cz], trio_final_matrix, feedforward_expand, feedforward_shrink)
    two = pair_tail(half, 0, parts, coupling_features, tri_own, weights)
    for part in range(parts - 1):
        two = pair_tail(1 - half, part, parts, coupling_features, tri_oth[part], weights, earlier=two)
    opm, pair = opm_block(
        left_res,
        right_all,
        product_final_matrix.reshape(outer, outer * cz),
        entry_order.T.astype(BF16),
        mine,
        two,
    )
    pair = pair_tail(
        1 - half, parts - 1, parts, coupling_features, tri_oth[-1], weights, opm=opm, earlier=pair
    )
    return (msa_out, pair)


def solution(mesh):


    return jax.shard_map(
        functools.partial(body, mesh.shape["row"]),
        mesh=mesh,
        in_specs=(
            P(("grp", "row"), None, None),
            P(("grp", "row"), None, None),
            P("grp", None),
            P("grp"),
            P(),
            P(),
            P(),
            P(),
            P(),
            P(),
            P(),
            P(),
            P(),
        ),
        out_specs=(P(("grp", "row"), None, None), P(("grp", "row"), None, None)),
        check_vma=False,
    )
```

```python
import functools

import jax
import jax.numpy as jnp
from jax import lax
from jax.experimental import pallas as pl
from jax.experimental.pallas import tpu as pltpu
from jax.sharding import PartitionSpec as P


EPSILON = 1e-05
F32 = jnp.float32
BF16 = jnp.bfloat16
LANES = 128
HEAD_UNROLL = 4
TAIL_UNROLL = 2
TAIL_ROWS = 8


def norm(values, axis=-1):
    centered = values - jnp.mean(values, axis=axis, keepdims=True)
    variance = jnp.mean(centered * centered, axis=axis, keepdims=True)
    return centered * lax.rsqrt(variance + EPSILON)


def dot(a, b, ca=1, cb=0):
    return lax.dot_general(a, b, (((ca,), (cb,)), ((), ())), preferred_element_type=F32)


def divisor(total, limit):
    best = min(total, limit)
    while total % best:
        best -= 1
    return best


def put_rows(scr, first, rows, values):
    for n in range(scr.shape[0]):
        scr[n, pl.ds(first, values.shape[0], stride=rows), :] = values[:, n * LANES : (n + 1) * LANES]


def get_rows(scr, first, rows):
    count = scr.shape[1] // rows
    return jnp.concatenate([scr[n, pl.ds(first, count, stride=rows), :] for n in range(scr.shape[0])], axis=1)


def full(shape):
    return pl.BlockSpec(shape, lambda *_: (0,) * len(shape))


def head_kernel(rows, with_bias, x_ref, vi_ref, vj_ref, w_ref, *refs):
    if with_bias:
        wb_ref, tri_ref, bias_ref, scr = refs
    else:
        tri_ref, scr = refs
    cz = x_ref.shape[2]
    heads = wb_ref.shape[0] if with_bias else 0

    def row(i, carry):
        xn = norm(x_ref[i].astype(F32)).astype(BF16)
        both = dot(w_ref[...], xn, 1, 1)
        valid = vj_ref[...] * vi_ref[0, i]
        put_rows(scr, i, rows, jax.nn.sigmoid(both[0:cz]) * both[cz : 2 * cz] * valid)
        if with_bias:
            put_rows(scr, cz * rows + i, rows, dot(wb_ref[...], xn, 1, 1))
        return carry

    lax.fori_loop(0, rows, row, 0, unroll=HEAD_UNROLL)
    for n in range(scr.shape[0]):
        cols = slice(n * LANES, (n + 1) * LANES)
        tri_ref[:, :, cols] = scr[n, 0 : cz * rows].astype(BF16).reshape(cz, rows, LANES)
        if with_bias:
            bias_ref[:, :, cols] = scr[n, cz * rows :].astype(BF16).reshape(heads, rows, LANES)


def pair_head(x, my_valid, valid, w, wb=None, part=0, parts=1):
    owned, res, cz = x.shape
    owned = owned // parts
    rows = divisor(owned, 16)
    steps = owned // rows
    heads = 0 if wb is None else wb.shape[0]
    in_specs = [
        pl.BlockSpec((rows, res, cz), lambda g: (g + part * steps, 0, 0)),
        pl.BlockSpec((1, 1, rows), lambda g: (g + part * steps, 0, 0), memory_space=pltpu.SMEM),
        full((1, res)),
        full(w.shape),
    ]
    args = [x, my_valid.reshape(-1, 1, rows), valid.reshape(1, res), w]
    out_specs = [pl.BlockSpec((cz, rows, res), lambda g: (0, g, 0))]
    out_shape = [jax.ShapeDtypeStruct((cz, owned, res), BF16)]
    if heads:
        in_specs.append(full(wb.shape))
        args.append(wb)
        out_specs.append(pl.BlockSpec((heads, rows, res), lambda g: (0, g, 0)))
        out_shape.append(jax.ShapeDtypeStruct((heads, owned, res), BF16))

    def kernel(x_ref, vi_ref, vj_ref, w_ref, *refs):
        head_kernel(rows, heads > 0, x_ref, vi_ref.at[0], vj_ref, w_ref, *refs)

    return pl.pallas_call(
        kernel,
        grid=(steps,),
        in_specs=in_specs,
        out_specs=out_specs,
        out_shape=out_shape,
        scratch_shapes=[pltpu.VMEM((res // LANES, (cz + heads) * rows, LANES), F32)],
        name="pair_head_bias" if heads else "pair_head",
    )(*args)


def msa_kernel(width, chunk, order, x_ref, valid_ref, bias_ref, w_ref, wf_ref, wp_ref, o_ref, l_ref, r_ref, q_s, k_s, v_s, att):
    res, feat = x_ref.shape[1:]
    half = feat // 2
    per_half = half // width
    x = x_ref[0].astype(F32)
    xn = norm(x).astype(BF16)
    q_s[...] = (dot(xn, w_ref[:, 0:feat]) * width ** (-0.5)).astype(BF16)
    k_s[...] = dot(xn, w_ref[:, feat : 2 * feat]).astype(BF16)
    v_s[...] = dot(xn, w_ref[:, 2 * feat : 3 * feat]).astype(BF16)
    valid = valid_ref[0]
    lane = lax.broadcasted_iota(jnp.int32, (1, feat), 1) // width
    lane_half = lax.broadcasted_iota(jnp.int32, (1, half), 1) // width

    def heads(step, carry):
        for side in (0, 1):
            mine = lane == step + side * per_half
            mine_half = lane_half == step
            v = jnp.where(mine, v_s[...], jnp.ones((), BF16))
            for c in range(res // chunk):
                span = slice(c * chunk, (c + 1) * chunk)
                q = jnp.where(mine, q_s[span], jnp.zeros((), BF16))
                lines = bias_ref.shape[2]
                owners = order[c * chunk // lines : (c + 1) * chunk // lines]
                bias = jnp.concatenate([bias_ref[g, step + side * per_half] for g in owners], axis=0)
                s = dot(q, k_s[...], 1, 1) + bias.astype(F32)
                s = jnp.where(valid > 0, s, -1000000000.0)
                p = jnp.exp(s - jnp.max(s, axis=1, keepdims=True)).astype(BF16)
                out = dot(p, v)
                mixed = out[:, side * half : (side + 1) * half] / out[:, (1 - side) * half : (2 - side) * half]
                cols = slice(side * half, (side + 1) * half)
                att[span, cols] = jnp.where(mine_half, mixed, att[span, cols])
        return carry

    lax.fori_loop(0, per_half, heads, 0)
    gate = jax.nn.sigmoid(dot(xn, w_ref[:, 3 * feat : 4 * feat]))
    mixed = (att[...] * gate).astype(BF16)
    new = x + dot(mixed, wf_ref[...])
    o_ref[0] = new.astype(BF16)
    factors = dot(wp_ref[...], norm(new).astype(BF16), 1, 1) * valid
    outer = l_ref.shape[1]
    l_ref[0] = factors[0:outer].astype(BF16)
    r_ref[0] = factors[outer : 2 * outer].astype(BF16)


def msa_block(x, valid, bias, order, w, wf, wp, width):
    seqs, res, feat = x.shape
    outer = wp.shape[0] // 2
    return pl.pallas_call(
        functools.partial(msa_kernel, width, divisor(res, 256), order),
        grid=(seqs,),
        in_specs=[
            pl.BlockSpec((1, res, feat), lambda s: (s, 0, 0)),
            pl.BlockSpec((1, 1, res), lambda s: (s, 0, 0)),
            full(bias.shape),
            full(w.shape),
            full(wf.shape),
            full(wp.shape),
        ],
        out_specs=[
            pl.BlockSpec((1, res, feat), lambda s: (s, 0, 0)),
            pl.BlockSpec((1, outer, res), lambda s: (s, 0, 0)),
            pl.BlockSpec((1, outer, res), lambda s: (s, 0, 0)),
        ],
        out_shape=[
            jax.ShapeDtypeStruct((seqs, res, feat), BF16),
            jax.ShapeDtypeStruct((seqs, outer, res), BF16),
            jax.ShapeDtypeStruct((seqs, outer, res), BF16),
        ],
        scratch_shapes=[pltpu.VMEM((res, feat), BF16)] * 3 + [pltpu.VMEM((res, feat), F32)],
        name="msa_block",
    )(x, valid.reshape(seqs, 1, res), bias, w, wf, wp)


def tri_kernel(l_ref, *refs):
    groups, chans, owned, res = l_ref.shape
    o_ref = refs[-1]
    for c in range(chans):
        a = l_ref[:, c].reshape(groups * owned, res)
        for n, r_ref in enumerate(refs[:-1]):
            count = groups * r_ref.shape[2]
            part = dot(a, r_ref[:, c].reshape(count, res), 1, 1).astype(BF16)
            o_ref[:, c, :, n * count : (n + 1) * count] = part.reshape(groups, owned, count)


def tri_sums(left, rights):
    groups, chans, owned, res = left.shape
    step = divisor(chans, 4)

    def spec(rows, cols):
        return pl.BlockSpec((groups, step, rows, cols), lambda c: (0, c, 0, 0))

    cols = groups * sum(r.shape[2] for r in rights)
    return pl.pallas_call(
        tri_kernel,
        grid=(chans // step,),
        in_specs=[spec(owned, res)] + [spec(r.shape[2], res) for r in rights],
        out_specs=spec(owned, cols),
        out_shape=jax.ShapeDtypeStruct((groups, chans, owned, cols), BF16),
        name="tri_sums",
    )(left, *rights)


def opm_kernel(l_ref, r_ref, w_ref, vt_ref, vi_ref, o_ref, mix, right):
    rows, seqs, outer = l_ref.shape
    owners, inner, local, res = r_ref.shape
    cz = o_ref.shape[2]
    depth = inner * local

    @pl.when(pl.program_id(0) == 0)
    def _():
        for g in range(owners):
            right[:, g * depth : (g + 1) * depth] = r_ref[g].reshape(depth, res).T

    many = max(16 // local, 1)
    for first in range(0, rows, 2):
        pair = min(2, rows - first)
        both = l_ref[first : first + pair].reshape(pair * seqs, outer)
        for d in range(0, inner, many):
            made = [dot(both, w_ref[:, (d + m) * cz : (d + m + 1) * cz]) for m in range(many)]
            for n in range(pair):
                for g in range(owners):
                    at = n * seqs + g * local
                    lines = jnp.concatenate([t[at : at + local] for t in made], axis=0).astype(BF16)
                    to = g * depth + d * local
                    mix[to : to + many * local, n * cz : (n + 1) * cz] = lines
        total = dot(right[...], mix[:, 0 : pair * cz])
        for n in range(pair):
            mine = jnp.broadcast_to(vi_ref[:, first + n : first + n + 1], (seqs, cz)).astype(BF16)
            tally = jnp.maximum(dot(vt_ref[...], mine), 1.0)
            o_ref[first + n] = total[:, n * cz : (n + 1) * cz] / tally


def opm_block(left, right, w, valid_t, mine):
    owned, seqs, outer = left.shape
    _, inner, _, res = right.shape
    cz = w.shape[1] // inner
    rows = divisor(owned, 8)
    pair = pl.BlockSpec((rows, res, cz), lambda g: (g, 0, 0))
    return pl.pallas_call(
        opm_kernel,
        grid=(owned // rows,),
        in_specs=[
            pl.BlockSpec((rows, seqs, outer), lambda g: (g, 0, 0)),
            full(right.shape),
            full(w.shape),
            full(valid_t.shape),
            pl.BlockSpec((None, seqs, rows), lambda g: (g, 0, 0)),
        ],
        out_specs=pair,
        out_shape=jax.ShapeDtypeStruct((owned, res, cz), F32),
        scratch_shapes=[pltpu.VMEM((seqs * inner, 2 * cz), BF16), pltpu.VMEM((res, seqs * inner), BF16)],
        name="opm_block",
    )(left, right, w, valid_t, mine.reshape(seqs, owned // rows, rows).transpose(1, 0, 2))


def tail_kernel(table_ref, x_ref, tri_ref, opm_ref, wg_ref, wt_ref, w1_ref, w2_ref, *refs):
    o_ref, scr = refs[-2:]
    rows, groups, lines, cz = x_ref.shape
    cols = groups * lines
    many = divisor(rows, TAIL_ROWS)
    for n in range(scr.shape[0]):
        part = tri_ref[:, :, n * LANES : (n + 1) * LANES]
        scr[n] = part.astype(F32).reshape(scr.shape[1:])

    def block(b, carry):
        i = b * many
        x = x_ref[pl.ds(i, many)].reshape(many * cols, cz).astype(F32)
        gate = jax.nn.sigmoid(dot(norm(x).astype(BF16), wg_ref[...]))
        tri = [dot(norm(get_rows(scr, i + m, rows), 0).astype(BF16), wt_ref[...], 0, 0) for m in range(many)]
        one = x + gate * jnp.concatenate(tri, axis=0)
        hidden = jnp.maximum(dot(norm(one).astype(BF16), w1_ref[...]), 0.0).astype(BF16)
        out = one + dot(hidden, w2_ref[...]) + opm_ref[pl.ds(i, many)].reshape(many * cols, cz)
        o_ref[pl.ds(i, many)] = out.astype(o_ref.dtype).reshape(many, groups, lines, cz)
        return carry

    lax.fori_loop(0, rows // many, block, 0, unroll=TAIL_UNROLL)


def pair_tail(table, parts, x, tri, opm, weights, earlier=None):
    owned, res, cz = x.shape
    ring = res // owned
    rows = divisor(owned, 16)
    lines = owned // parts
    span = ring // 2 * lines
    view = (owned, ring, parts, lines, cz)
    pair = pl.BlockSpec((rows, ring // 2, None, lines, cz), lambda q, g, t: (g, t[0, q], t[1, q], 0, 0))
    in_specs = [pair, pl.BlockSpec((cz, rows, span), lambda q, g, t: (0, g, q)), pair]
    in_specs += [full(w.shape) for w in weights]
    args = [table, x.reshape(view), tri, opm.reshape(view), *weights]
    aliases = {}
    if earlier is not None:
        aliases = {len(args): 0}
        in_specs.append(pl.BlockSpec(memory_space=pl.ANY))
        args.append(earlier.reshape(view))
    return pl.pallas_call(
        tail_kernel,
        grid_spec=pltpu.PrefetchScalarGridSpec(
            num_scalar_prefetch=1,
            grid=(tri.shape[2] // span, owned // rows),
            in_specs=in_specs,
            out_specs=pair,
            scratch_shapes=[pltpu.VMEM((max(span // LANES, 1), cz * rows, min(span, LANES)), F32)],
        ),
        out_shape=jax.ShapeDtypeStruct(view, BF16),
        input_output_aliases=aliases,
        name="pair_tail",
    )(*args).reshape(owned, res, cz)


def body(
    ring,
    coupling_features,
    aligned_features,
    aligned_entry_flags,
    amino_real_flags,
    coupling_offset_matrix,
    lookup_matrices,
    aligned_final_matrix,
    product_factor_matrices,
    product_final_matrix,
    trio_factor_matrices,
    trio_final_matrix,
    feedforward_expand,
    feedforward_shrink,
):
    owned, res, cz = coupling_features.shape
    seqs, _, feat = aligned_features.shape
    width = feat // coupling_offset_matrix.shape[1]
    outer = product_factor_matrices.shape[1] // 2
    place = lax.axis_index("row")
    near = ring // 2
    halves = [list(range(near)), list(range(near, ring))]
    swap = [(r, (r + near) % ring) for r in range(ring)]

    residue = amino_real_flags.astype(F32)
    entry = aligned_entry_flags.astype(F32) * residue[None, :]
    my_residue = lax.dynamic_slice_in_dim(residue, place * owned, owned, 0)
    my_entry = lax.dynamic_slice_in_dim(entry, place * seqs, seqs, 0)
    trio = trio_factor_matrices.T

    parts = 2 if owned % 32 == 0 else 1
    half = (place // near).astype(jnp.int32)

    def spread(values):
        values = values.reshape(near, cz // near, values.shape[1], values.shape[-1])
        return lax.all_to_all(values, "row", 0, 0, tiled=True, axis_index_groups=halves)

    made = [
        pair_head(coupling_features, my_residue, residue, trio[2 * cz : 4 * cz], coupling_offset_matrix.T, part, parts)
        for part in range(parts)
    ]
    bias = jnp.concatenate([b for _, b in made], axis=1)

    planes = 4 if ring % 4 == 0 else 1
    members = ring // planes
    plane = place // members
    within = [[m + members * z for m in range(members)] for z in range(planes)]
    order = [m * planes + z for z in range(planes) for m in range(members)]

    def across(values):
        got = [values[0]]
        for k in range(1, planes):
            got.append(lax.ppermute(values[k], "row", [(r, r ^ (k * members)) for r in range(ring)]))
        got = jnp.stack(got)
        return jnp.stack([lax.dynamic_index_in_dim(got, plane ^ z, 0, keepdims=False) for z in range(planes)])

    def gather(values):
        values = lax.all_gather(values, "row", axis=0, axis_index_groups=within)
        return values.reshape((ring,) + values.shape[2:])

    bias = across([bias] * planes)
    right_own, right_oth = [], []
    for part in range(parts):
        right = made[part][0]
        if part:
            right, bias = lax.optimization_barrier((right, bias))
        right_own.append(spread(right))
        right_oth.append(lax.ppermute(right_own[part], "row", swap))
    (left,) = pair_head(coupling_features, my_residue, residue, trio[0 : 2 * cz])
    left_own = spread(left)
    bias_all = gather(bias)

    msa_out, left_opm, right_opm = msa_block(
        aligned_features,
        my_entry,
        bias_all,
        order,
        lookup_matrices,
        aligned_final_matrix,
        product_factor_matrices.T,
        width,
    )

    def collect(sums):
        back = lax.all_to_all(sums, "row", 0, 0, tiled=True, axis_index_groups=halves)
        return back.reshape(cz, owned, sums.shape[-1])

    spot = res // planes
    both = []
    for k in range(planes):
        lines = lax.dynamic_slice_in_dim(left_opm, (plane ^ k) * spot, spot, 2)
        both.append(jnp.concatenate([right_opm, lines], axis=2).transpose(1, 0, 2))
    both = gather(across(both))
    right_all = both[..., 0:res]
    left_res = lax.dynamic_slice_in_dim(both, res + (place % members) * owned, owned, 3)
    left_res = left_res.transpose(3, 0, 2, 1).reshape(owned, ring * seqs, outer)
    entry_order = entry.reshape(planes, members, seqs, res).transpose(1, 0, 2, 3).reshape(ring * seqs, res)
    mine = lax.dynamic_slice_in_dim(entry_order, place * owned, owned, 1)
    opm = opm_block(
        left_res,
        right_all,
        product_final_matrix.reshape(outer, outer * cz),
        entry_order.T.astype(BF16),
        mine,
    )

    sums = tri_sums(left_own, right_own + right_oth[:-1])
    tri_near = collect(sums)
    sums = tri_sums(left_own, right_oth[-1:])
    tri_last = collect(sums)
    weights = (trio_factor_matrices[:, 4 * cz : 5 * cz], trio_final_matrix, feedforward_expand, feedforward_shrink)
    table = jnp.array([[0] * parts + [1] * parts, list(range(parts)) * 2], jnp.int32)
    table = table.at[0].set(table[0] ^ half)
    pair = pair_tail(table[:, :-1], parts, coupling_features, tri_near, opm, weights)
    pair = pair_tail(table[:, -1:], parts, coupling_features, tri_last, opm, weights, earlier=pair)
    return (msa_out, pair)


def solution(mesh):


    return jax.shard_map(
        functools.partial(body, mesh.shape["row"]),
        mesh=mesh,
        in_specs=(
            P(("grp", "row"), None, None),
            P(("grp", "row"), None, None),
            P("grp", None),
            P("grp"),
            P(),
            P(),
            P(),
            P(),
            P(),
            P(),
            P(),
            P(),
            P(),
        ),
        out_specs=(P(("grp", "row"), None, None), P(("grp", "row"), None, None)),
        check_vma=False,
    )
```

```python
import functools

import jax
import jax.numpy as jnp
from jax import lax
from jax.experimental import pallas as pl
from jax.experimental.pallas import tpu as pltpu
from jax.sharding import PartitionSpec as P


EPSILON = 1e-05
F32 = jnp.float32
BF16 = jnp.bfloat16
LANES = 128
HEAD_UNROLL = 4
TAIL_UNROLL = 2
TAIL_ROWS = 8


def norm(values, axis=-1):
    centered = values - jnp.mean(values, axis=axis, keepdims=True)
    variance = jnp.mean(centered * centered, axis=axis, keepdims=True)
    return centered * lax.rsqrt(variance + EPSILON)


def dot(a, b, ca=1, cb=0):
    return lax.dot_general(a, b, (((ca,), (cb,)), ((), ())), preferred_element_type=F32)


def divisor(total, limit):
    best = min(total, limit)
    while total % best:
        best -= 1
    return best


def put_rows(scr, first, rows, values):
    for n in range(scr.shape[0]):
        scr[n, pl.ds(first, values.shape[0], stride=rows), :] = values[:, n * LANES : (n + 1) * LANES]


def get_rows(scr, first, rows):
    count = scr.shape[1] // rows
    return jnp.concatenate([scr[n, pl.ds(first, count, stride=rows), :] for n in range(scr.shape[0])], axis=1)


def full(shape):
    return pl.BlockSpec(shape, lambda *_: (0,) * len(shape))


def bias_kernel(x_ref, w_ref, o_ref, scr):
    rows = x_ref.shape[0]
    heads = w_ref.shape[0]

    def row(i, carry):
        xn = norm(x_ref[i].astype(F32)).astype(BF16)
        put_rows(scr, i, rows, dot(w_ref[...], xn, 1, 1))
        return carry

    lax.fori_loop(0, rows, row, 0, unroll=HEAD_UNROLL)
    for n in range(scr.shape[0]):
        o_ref[:, :, n * LANES : (n + 1) * LANES] = scr[n].astype(BF16).reshape(heads, rows, LANES)


def pair_bias(x, w):
    owned, res, cz = x.shape
    rows = divisor(owned, 16)
    heads = w.shape[0]
    return pl.pallas_call(
        bias_kernel,
        grid=(owned // rows,),
        in_specs=[pl.BlockSpec((rows, res, cz), lambda g: (g, 0, 0)), full(w.shape)],
        out_specs=pl.BlockSpec((heads, rows, res), lambda g: (0, g, 0)),
        out_shape=jax.ShapeDtypeStruct((heads, owned, res), BF16),
        scratch_shapes=[pltpu.VMEM((res // LANES, heads * rows, LANES), F32)],
        name="pair_bias",
    )(x, w)


def head_kernel(x_ref, vi_ref, vj_ref, w_ref, tri_ref, scr):
    rows, _, cz = x_ref.shape

    def row(i, carry):
        xn = norm(x_ref[i].astype(F32)).astype(BF16)
        both = dot(w_ref[...], xn, 1, 1)
        valid = vj_ref[...] * vi_ref[0, 0, i]
        put_rows(scr, i, rows, jax.nn.sigmoid(both[0:cz]) * both[cz : 2 * cz] * valid)
        return carry

    lax.fori_loop(0, rows, row, 0, unroll=HEAD_UNROLL)
    for n in range(scr.shape[0]):
        tri_ref[:, :, n * LANES : (n + 1) * LANES] = scr[n].astype(BF16).reshape(cz, rows, LANES)


def pair_head(x, my_valid, valid, w, part=0, parts=1):
    owned, res, cz = x.shape
    owned = owned // parts
    rows = divisor(owned, 16)
    steps = owned // rows
    return pl.pallas_call(
        head_kernel,
        grid=(steps,),
        in_specs=[
            pl.BlockSpec((rows, res, cz), lambda g: (g + part * steps, 0, 0)),
            pl.BlockSpec((1, 1, rows), lambda g: (g + part * steps, 0, 0), memory_space=pltpu.SMEM),
            full((1, res)),
            full(w.shape),
        ],
        out_specs=pl.BlockSpec((cz, rows, res), lambda g: (0, g, 0)),
        out_shape=jax.ShapeDtypeStruct((cz, owned, res), BF16),
        scratch_shapes=[pltpu.VMEM((res // LANES, cz * rows, LANES), F32)],
        name="pair_head",
    )(x, my_valid.reshape(-1, 1, rows), valid.reshape(1, res), w)


def msa_kernel(width, chunk, order, x_ref, valid_ref, bias_ref, w_ref, wf_ref, wp_ref, o_ref, l_ref, r_ref, q_s, k_s, v_s, att):
    res, feat = x_ref.shape[1:]
    half = feat // 2
    per_half = half // width
    x = x_ref[0].astype(F32)
    xn = norm(x).astype(BF16)
    q_s[...] = (dot(xn, w_ref[:, 0:feat]) * width ** (-0.5)).astype(BF16)
    k_s[...] = dot(xn, w_ref[:, feat : 2 * feat]).astype(BF16)
    v_s[...] = dot(xn, w_ref[:, 2 * feat : 3 * feat]).astype(BF16)
    valid = valid_ref[0]
    lane = lax.broadcasted_iota(jnp.int32, (1, feat), 1) // width
    lane_half = lax.broadcasted_iota(jnp.int32, (1, half), 1) // width

    def heads(step, carry):
        for side in (0, 1):
            mine = lane == step + side * per_half
            mine_half = lane_half == step
            v = jnp.where(mine, v_s[...], jnp.ones((), BF16))
            for c in range(res // chunk):
                span = slice(c * chunk, (c + 1) * chunk)
                q = jnp.where(mine, q_s[span], jnp.zeros((), BF16))
                lines = bias_ref.shape[2]
                owners = order[c * chunk // lines : (c + 1) * chunk // lines]
                bias = jnp.concatenate([bias_ref[g, step + side * per_half] for g in owners], axis=0)
                s = dot(q, k_s[...], 1, 1) + bias.astype(F32)
                s = jnp.where(valid > 0, s, -1000000000.0)
                p = jnp.exp(s - jnp.max(s, axis=1, keepdims=True)).astype(BF16)
                out = dot(p, v)
                mixed = out[:, side * half : (side + 1) * half] / out[:, (1 - side) * half : (2 - side) * half]
                cols = slice(side * half, (side + 1) * half)
                att[span, cols] = jnp.where(mine_half, mixed, att[span, cols])
        return carry

    lax.fori_loop(0, per_half, heads, 0)
    gate = jax.nn.sigmoid(dot(xn, w_ref[:, 3 * feat : 4 * feat]))
    mixed = (att[...] * gate).astype(BF16)
    new = x + dot(mixed, wf_ref[...])
    o_ref[0] = new.astype(BF16)
    factors = dot(wp_ref[...], norm(new).astype(BF16), 1, 1) * valid
    outer = l_ref.shape[1]
    l_ref[0] = factors[0:outer].astype(BF16)
    r_ref[0] = factors[outer : 2 * outer].astype(BF16)


def msa_block(x, valid, bias, order, w, wf, wp, width):
    seqs, res, feat = x.shape
    outer = wp.shape[0] // 2
    return pl.pallas_call(
        functools.partial(msa_kernel, width, divisor(res, 256), order),
        grid=(seqs,),
        in_specs=[
            pl.BlockSpec((1, res, feat), lambda s: (s, 0, 0)),
            pl.BlockSpec((1, 1, res), lambda s: (s, 0, 0)),
            full(bias.shape),
            full(w.shape),
            full(wf.shape),
            full(wp.shape),
        ],
        out_specs=[
            pl.BlockSpec((1, res, feat), lambda s: (s, 0, 0)),
            pl.BlockSpec((1, outer, res), lambda s: (s, 0, 0)),
            pl.BlockSpec((1, outer, res), lambda s: (s, 0, 0)),
        ],
        out_shape=[
            jax.ShapeDtypeStruct((seqs, res, feat), BF16),
            jax.ShapeDtypeStruct((seqs, outer, res), BF16),
            jax.ShapeDtypeStruct((seqs, outer, res), BF16),
        ],
        scratch_shapes=[pltpu.VMEM((res, feat), BF16)] * 3 + [pltpu.VMEM((res, feat), F32)],
        name="msa_block",
    )(x, valid.reshape(seqs, 1, res), bias, w, wf, wp)


def tri_kernel(l_ref, *refs):
    groups, chans, owned, res = l_ref.shape
    o_ref = refs[-1]
    for c in range(chans):
        a = l_ref[:, c].reshape(groups * owned, res)
        for n, r_ref in enumerate(refs[:-1]):
            count = groups * r_ref.shape[2]
            part = dot(a, r_ref[:, c].reshape(count, res), 1, 1).astype(BF16)
            o_ref[:, c, :, n * count : (n + 1) * count] = part.reshape(groups, owned, count)


def tri_sums(left, rights):
    groups, chans, owned, res = left.shape
    step = divisor(chans, 4)

    def spec(rows, cols):
        return pl.BlockSpec((groups, step, rows, cols), lambda c: (0, c, 0, 0))

    cols = groups * sum(r.shape[2] for r in rights)
    return pl.pallas_call(
        tri_kernel,
        grid=(chans // step,),
        in_specs=[spec(owned, res)] + [spec(r.shape[2], res) for r in rights],
        out_specs=spec(owned, cols),
        out_shape=jax.ShapeDtypeStruct((groups, chans, owned, cols), BF16),
        name="tri_sums",
    )(left, *rights)


def opm_kernel(l_ref, r_ref, w_ref, vt_ref, vi_ref, o_ref, mix, right):
    rows, seqs, outer = l_ref.shape
    owners, inner, local, _ = r_ref.shape
    res, cz = o_ref.shape[1:]
    depth = inner * local

    @pl.when(pl.program_id(0) == 0)
    def _():
        for g in range(owners):
            right[:, g * depth : (g + 1) * depth] = r_ref[g, :, :, 0:res].reshape(depth, res).T

    many = max(16 // local, 1)
    for first in range(0, rows, 2):
        pair = min(2, rows - first)
        both = l_ref[first : first + pair].reshape(pair * seqs, outer)
        for d in range(0, inner, many):
            made = [dot(both, w_ref[:, (d + m) * cz : (d + m + 1) * cz]) for m in range(many)]
            for n in range(pair):
                for g in range(owners):
                    at = n * seqs + g * local
                    lines = jnp.concatenate([t[at : at + local] for t in made], axis=0).astype(BF16)
                    to = g * depth + d * local
                    mix[to : to + many * local, n * cz : (n + 1) * cz] = lines
        total = dot(right[...], mix[:, 0 : pair * cz])
        for n in range(pair):
            mine = jnp.broadcast_to(vi_ref[:, first + n : first + n + 1], (seqs, cz)).astype(BF16)
            tally = jnp.maximum(dot(vt_ref[...], mine), 1.0)
            o_ref[first + n] = total[:, n * cz : (n + 1) * cz] / tally


def opm_block(left, right, w, valid_t, mine):
    owned, seqs, outer = left.shape
    _, inner, _, _ = right.shape
    res = valid_t.shape[0]
    cz = w.shape[1] // inner
    rows = divisor(owned, 8)
    pair = pl.BlockSpec((rows, res, cz), lambda g: (g, 0, 0))
    return pl.pallas_call(
        opm_kernel,
        grid=(owned // rows,),
        in_specs=[
            pl.BlockSpec((rows, seqs, outer), lambda g: (g, 0, 0)),
            full(right.shape),
            full(w.shape),
            full(valid_t.shape),
            pl.BlockSpec((None, seqs, rows), lambda g: (g, 0, 0)),
        ],
        out_specs=pair,
        out_shape=jax.ShapeDtypeStruct((owned, res, cz), F32),
        scratch_shapes=[pltpu.VMEM((seqs * inner, 2 * cz), BF16), pltpu.VMEM((res, seqs * inner), BF16)],
        name="opm_block",
    )(left, right, w, valid_t, mine.reshape(seqs, owned // rows, rows).transpose(1, 0, 2))


def tail_kernel(table_ref, x_ref, tri_ref, opm_ref, wg_ref, wt_ref, w1_ref, w2_ref, *refs):
    o_ref, scr = refs[-2:]
    rows, groups, lines, cz = x_ref.shape
    cols = groups * lines
    many = divisor(rows, TAIL_ROWS)
    for n in range(scr.shape[0]):
        part = tri_ref[:, :, n * LANES : (n + 1) * LANES]
        scr[n] = part.astype(F32).reshape(scr.shape[1:])

    def block(b, carry):
        i = b * many
        x = x_ref[pl.ds(i, many)].reshape(many * cols, cz).astype(F32)
        gate = jax.nn.sigmoid(dot(norm(x).astype(BF16), wg_ref[...]))
        tri = [dot(norm(get_rows(scr, i + m, rows), 0).astype(BF16), wt_ref[...], 0, 0) for m in range(many)]
        one = x + gate * jnp.concatenate(tri, axis=0)
        hidden = jnp.maximum(dot(norm(one).astype(BF16), w1_ref[...]), 0.0).astype(BF16)
        out = one + dot(hidden, w2_ref[...]) + opm_ref[pl.ds(i, many)].reshape(many * cols, cz)
        o_ref[pl.ds(i, many)] = out.astype(o_ref.dtype).reshape(many, groups, lines, cz)
        return carry

    lax.fori_loop(0, rows // many, block, 0, unroll=TAIL_UNROLL)


def pair_tail(table, parts, x, tri, opm, weights, earlier=None):
    owned, res, cz = x.shape
    ring = res // owned
    rows = divisor(owned, 16)
    lines = owned // parts
    span = ring // 2 * lines
    view = (owned, ring, parts, lines, cz)
    pair = pl.BlockSpec((rows, ring // 2, None, lines, cz), lambda q, g, t: (g, t[0, q], t[1, q], 0, 0))
    in_specs = [pair, pl.BlockSpec((cz, rows, span), lambda q, g, t: (0, g, q)), pair]
    in_specs += [full(w.shape) for w in weights]
    args = [table, x.reshape(view), tri, opm.reshape(view), *weights]
    aliases = {}
    if earlier is not None:
        aliases = {len(args): 0}
        in_specs.append(pl.BlockSpec(memory_space=pl.ANY))
        args.append(earlier.reshape(view))
    return pl.pallas_call(
        tail_kernel,
        grid_spec=pltpu.PrefetchScalarGridSpec(
            num_scalar_prefetch=1,
            grid=(tri.shape[2] // span, owned // rows),
            in_specs=in_specs,
            out_specs=pair,
            scratch_shapes=[pltpu.VMEM((max(span // LANES, 1), cz * rows, min(span, LANES)), F32)],
        ),
        out_shape=jax.ShapeDtypeStruct(view, BF16),
        input_output_aliases=aliases,
        name="pair_tail",
    )(*args).reshape(owned, res, cz)


def body(
    ring,
    coupling_features,
    aligned_features,
    aligned_entry_flags,
    amino_real_flags,
    coupling_offset_matrix,
    lookup_matrices,
    aligned_final_matrix,
    product_factor_matrices,
    product_final_matrix,
    trio_factor_matrices,
    trio_final_matrix,
    feedforward_expand,
    feedforward_shrink,
):
    owned, res, cz = coupling_features.shape
    seqs, _, feat = aligned_features.shape
    width = feat // coupling_offset_matrix.shape[1]
    outer = product_factor_matrices.shape[1] // 2
    place = lax.axis_index("row")
    near = ring // 2
    halves = [list(range(near)), list(range(near, ring))]
    swap = [(r, (r + near) % ring) for r in range(ring)]

    residue = amino_real_flags.astype(F32)
    entry = aligned_entry_flags.astype(F32) * residue[None, :]
    my_residue = lax.dynamic_slice_in_dim(residue, place * owned, owned, 0)
    my_entry = lax.dynamic_slice_in_dim(entry, place * seqs, seqs, 0)
    trio = trio_factor_matrices.T

    parts = 2 if owned % 32 == 0 else 1
    half = (place // near).astype(jnp.int32)

    def spread(values):
        values = values.reshape(near, cz // near, values.shape[1], values.shape[-1])
        return lax.all_to_all(values, "row", 0, 0, tiled=True, axis_index_groups=halves)

    bias = pair_bias(coupling_features, coupling_offset_matrix.T)
    made = []
    for part in range(parts):
        made.append(
            pair_head(coupling_features, my_residue, residue, trio[2 * cz : 4 * cz], part, parts)
        )

    planes = 4 if ring % 4 == 0 else 1
    members = ring // planes
    plane = place // members
    within = [[m + members * z for m in range(members)] for z in range(planes)]
    order = [m * planes + z for z in range(planes) for m in range(members)]

    def across(values):
        got = [values[0]]
        for k in range(1, planes):
            got.append(lax.ppermute(values[k], "row", [(r, r ^ (k * members)) for r in range(ring)]))
        got = jnp.stack(got)
        return jnp.stack([lax.dynamic_index_in_dim(got, plane ^ z, 0, keepdims=False) for z in range(planes)])

    def gather(values):
        values = lax.all_gather(values, "row", axis=0, axis_index_groups=within)
        return values.reshape((ring,) + values.shape[2:])

    bias = across([bias] * planes)
    right_own, right_oth = [], []
    for part in range(parts):
        right = made[part]
        right_own.append(spread(right))
        right_oth.append(lax.ppermute(right_own[part], "row", swap))
    left = pair_head(coupling_features, my_residue, residue, trio[0 : 2 * cz])
    left, bias = lax.optimization_barrier((left, bias))
    left_own = spread(left)
    bias_all = gather(bias)

    msa_out, left_opm, right_opm = msa_block(
        aligned_features,
        my_entry,
        bias_all,
        order,
        lookup_matrices,
        aligned_final_matrix,
        product_factor_matrices.T,
        width,
    )

    def collect(sums):
        back = lax.all_to_all(sums, "row", 0, 0, tiled=True, axis_index_groups=halves)
        return back.reshape(cz, owned, sums.shape[-1])

    spot = res // planes
    both = []
    for k in range(planes):
        lines = lax.dynamic_slice_in_dim(left_opm, (plane ^ k) * spot, spot, 2)
        both.append(jnp.concatenate([right_opm, lines], axis=2).transpose(1, 0, 2))
    both = gather(across(both))
    left_res = lax.dynamic_slice_in_dim(both, res + (place % members) * owned, owned, 3)
    left_res = left_res.transpose(3, 0, 2, 1).reshape(owned, ring * seqs, outer)
    entry_order = entry.reshape(planes, members, seqs, res).transpose(1, 0, 2, 3).reshape(ring * seqs, res)
    mine = lax.dynamic_slice_in_dim(entry_order, place * owned, owned, 1)
    opm = opm_block(left_res, both, product_final_matrix.reshape(outer, outer * cz), entry_order.T.astype(BF16), mine)

    sums = tri_sums(left_own, right_own + right_oth[:-1])
    tri_near = collect(sums)
    sums = tri_sums(left_own, right_oth[-1:])
    tri_last = collect(sums)
    weights = (trio_factor_matrices[:, 4 * cz : 5 * cz], trio_final_matrix, feedforward_expand, feedforward_shrink)
    table = jnp.array([[0] * parts + [1] * parts, list(range(parts)) * 2], jnp.int32)
    table = table.at[0].set(table[0] ^ half)
    pair = pair_tail(table[:, :-1], parts, coupling_features, tri_near, opm, weights)
    pair = pair_tail(table[:, -1:], parts, coupling_features, tri_last, opm, weights, earlier=pair)
    return (msa_out, pair)


def solution(mesh):


    return jax.shard_map(
        functools.partial(body, mesh.shape["row"]),
        mesh=mesh,
        in_specs=(
            P(("grp", "row"), None, None),
            P(("grp", "row"), None, None),
            P("grp", None),
            P("grp"),
            P(),
            P(),
            P(),
            P(),
            P(),
            P(),
            P(),
            P(),
            P(),
        ),
        out_specs=(P(("grp", "row"), None, None), P(("grp", "row"), None, None)),
        check_vma=False,
    )
```

```python
import functools

import jax
import jax.numpy as jnp
from jax import lax
from jax.experimental import pallas as pl
from jax.experimental.pallas import tpu as pltpu
from jax.sharding import PartitionSpec as P


EPSILON = 1e-05
F32 = jnp.float32
BF16 = jnp.bfloat16
LANES = 128
HEAD_UNROLL = 8
TAIL_UNROLL = 2
TAIL_ROWS = 8


def norm(values, axis=-1):
    centered = values - jnp.mean(values, axis=axis, keepdims=True)
    variance = jnp.mean(centered * centered, axis=axis, keepdims=True)
    return centered * lax.rsqrt(variance + EPSILON)


def dot(a, b, ca=1, cb=0):
    return lax.dot_general(a, b, (((ca,), (cb,)), ((), ())), preferred_element_type=F32)


def divisor(total, limit):
    best = min(total, limit)
    while total % best:
        best -= 1
    return best


def put_rows(scr, first, rows, values):
    for n in range(scr.shape[0]):
        scr[n, pl.ds(first, values.shape[0], stride=rows), :] = values[:, n * LANES : (n + 1) * LANES]


def get_rows(scr, first, rows):
    count = scr.shape[1] // rows
    return jnp.concatenate([scr[n, pl.ds(first, count, stride=rows), :] for n in range(scr.shape[0])], axis=1)


def full(shape):
    return pl.BlockSpec(shape, lambda *_: (0,) * len(shape))


def bias_kernel(x_ref, w_ref, o_ref, scr):
    rows = x_ref.shape[0]
    heads = w_ref.shape[0]

    def row(i, carry):
        xn = norm(x_ref[i].astype(F32)).astype(BF16)
        put_rows(scr, i, rows, dot(w_ref[...], xn, 1, 1))
        return carry

    lax.fori_loop(0, rows, row, 0, unroll=HEAD_UNROLL)
    for n in range(scr.shape[0]):
        o_ref[:, :, n * LANES : (n + 1) * LANES] = scr[n].astype(BF16).reshape(heads, rows, LANES)


def pair_bias(x, w):
    owned, res, cz = x.shape
    rows = divisor(owned, 16)
    heads = w.shape[0]
    return pl.pallas_call(
        bias_kernel,
        grid=(owned // rows,),
        in_specs=[pl.BlockSpec((rows, res, cz), lambda g: (g, 0, 0)), full(w.shape)],
        out_specs=pl.BlockSpec((heads, rows, res), lambda g: (0, g, 0)),
        out_shape=jax.ShapeDtypeStruct((heads, owned, res), BF16),
        scratch_shapes=[pltpu.VMEM((res // LANES, heads * rows, LANES), F32)],
        name="pair_bias",
    )(x, w)


def head_kernel(x_ref, vi_ref, vj_ref, w_ref, tri_ref, scr):
    rows, _, cz = x_ref.shape

    def row(i, carry):
        xn = norm(x_ref[i].astype(F32)).astype(BF16)
        both = dot(w_ref[...], xn, 1, 1)
        valid = vj_ref[...] * vi_ref[0, 0, i]
        put_rows(scr, i, rows, jax.nn.sigmoid(both[0:cz]) * both[cz : 2 * cz] * valid)
        return carry

    lax.fori_loop(0, rows, row, 0, unroll=HEAD_UNROLL)
    for n in range(scr.shape[0]):
        tri_ref[:, :, n * LANES : (n + 1) * LANES] = scr[n].astype(BF16).reshape(cz, rows, LANES)


def pair_head(x, my_valid, valid, w, part=0, parts=1):
    owned, res, cz = x.shape
    owned = owned // parts
    rows = divisor(owned, 16)
    steps = owned // rows
    return pl.pallas_call(
        head_kernel,
        grid=(steps,),
        in_specs=[
            pl.BlockSpec((rows, res, cz), lambda g: (g + part * steps, 0, 0)),
            pl.BlockSpec((1, 1, rows), lambda g: (g + part * steps, 0, 0), memory_space=pltpu.SMEM),
            full((1, res)),
            full(w.shape),
        ],
        out_specs=pl.BlockSpec((cz, rows, res), lambda g: (0, g, 0)),
        out_shape=jax.ShapeDtypeStruct((cz, owned, res), BF16),
        scratch_shapes=[pltpu.VMEM((res // LANES, cz * rows, LANES), F32)],
        name="pair_head",
    )(x, my_valid.reshape(-1, 1, rows), valid.reshape(1, res), w)


def msa_kernel(width, chunk, order, x_ref, valid_ref, bias_ref, w_ref, wf_ref, wp_ref, o_ref, l_ref, r_ref, q_s, k_s, v_s, att):
    res, feat = x_ref.shape[1:]
    half = feat // 2
    per_half = half // width
    x = x_ref[0].astype(F32)
    xn = norm(x).astype(BF16)
    q_s[...] = (dot(xn, w_ref[:, 0:feat]) * width ** (-0.5)).astype(BF16)
    k_s[...] = dot(xn, w_ref[:, feat : 2 * feat]).astype(BF16)
    v_s[...] = dot(xn, w_ref[:, 2 * feat : 3 * feat]).astype(BF16)
    valid = valid_ref[0]
    lane = lax.broadcasted_iota(jnp.int32, (1, feat), 1) // width
    lane_half = lax.broadcasted_iota(jnp.int32, (1, half), 1) // width

    def heads(step, carry):
        for side in (0, 1):
            mine = lane == step + side * per_half
            mine_half = lane_half == step
            v = jnp.where(mine, v_s[...], jnp.ones((), BF16))
            for c in range(res // chunk):
                span = slice(c * chunk, (c + 1) * chunk)
                q = jnp.where(mine, q_s[span], jnp.zeros((), BF16))
                lines = bias_ref.shape[2]
                owners = order[c * chunk // lines : (c + 1) * chunk // lines]
                bias = jnp.concatenate([bias_ref[g, step + side * per_half] for g in owners], axis=0)
                s = dot(q, k_s[...], 1, 1) + bias.astype(F32)
                s = jnp.where(valid > 0, s, -1000000000.0)
                p = jnp.exp(s - jnp.max(s, axis=1, keepdims=True)).astype(BF16)
                out = dot(p, v)
                mixed = out[:, side * half : (side + 1) * half] / out[:, (1 - side) * half : (2 - side) * half]
                cols = slice(side * half, (side + 1) * half)
                att[span, cols] = jnp.where(mine_half, mixed, att[span, cols])
        return carry

    lax.fori_loop(0, per_half, heads, 0)
    gate = jax.nn.sigmoid(dot(xn, w_ref[:, 3 * feat : 4 * feat]))
    mixed = (att[...] * gate).astype(BF16)
    new = x + dot(mixed, wf_ref[...])
    o_ref[0] = new.astype(BF16)
    factors = dot(wp_ref[...], norm(new).astype(BF16), 1, 1) * valid
    outer = l_ref.shape[1]
    l_ref[0] = factors[0:outer].astype(BF16)
    r_ref[0] = factors[outer : 2 * outer].astype(BF16)


def msa_block(x, valid, bias, order, w, wf, wp, width):
    seqs, res, feat = x.shape
    outer = wp.shape[0] // 2
    return pl.pallas_call(
        functools.partial(msa_kernel, width, divisor(res, 256), order),
        grid=(seqs,),
        in_specs=[
            pl.BlockSpec((1, res, feat), lambda s: (s, 0, 0)),
            pl.BlockSpec((1, 1, res), lambda s: (s, 0, 0)),
            full(bias.shape),
            full(w.shape),
            full(wf.shape),
            full(wp.shape),
        ],
        out_specs=[
            pl.BlockSpec((1, res, feat), lambda s: (s, 0, 0)),
            pl.BlockSpec((1, outer, res), lambda s: (s, 0, 0)),
            pl.BlockSpec((1, outer, res), lambda s: (s, 0, 0)),
        ],
        out_shape=[
            jax.ShapeDtypeStruct((seqs, res, feat), BF16),
            jax.ShapeDtypeStruct((seqs, outer, res), BF16),
            jax.ShapeDtypeStruct((seqs, outer, res), BF16),
        ],
        scratch_shapes=[pltpu.VMEM((res, feat), BF16)] * 3 + [pltpu.VMEM((res, feat), F32)],
        name="msa_block",
    )(x, valid.reshape(seqs, 1, res), bias, w, wf, wp)


def tri_kernel(l_ref, *refs):
    groups, chans, owned, res = l_ref.shape
    o_ref = refs[-1]
    for c in range(chans):
        a = l_ref[:, c].reshape(groups * owned, res)
        for n, r_ref in enumerate(refs[:-1]):
            count = groups * r_ref.shape[2]
            part = dot(a, r_ref[:, c].reshape(count, res), 1, 1).astype(BF16)
            o_ref[:, c, :, n * count : (n + 1) * count] = part.reshape(groups, owned, count)


def tri_sums(left, rights):
    groups, chans, owned, res = left.shape
    step = divisor(chans, 4)

    def spec(rows, cols):
        return pl.BlockSpec((groups, step, rows, cols), lambda c: (0, c, 0, 0))

    cols = groups * sum(r.shape[2] for r in rights)
    return pl.pallas_call(
        tri_kernel,
        grid=(chans // step,),
        in_specs=[spec(owned, res)] + [spec(r.shape[2], res) for r in rights],
        out_specs=spec(owned, cols),
        out_shape=jax.ShapeDtypeStruct((groups, chans, owned, cols), BF16),
        name="tri_sums",
    )(left, *rights)


def opm_kernel(l_ref, r_ref, w_ref, vt_ref, vi_ref, o_ref, mix, right):
    rows, seqs, outer = l_ref.shape
    owners, inner, local, _ = r_ref.shape
    res, cz = o_ref.shape[1:]
    depth = inner * local

    @pl.when(pl.program_id(0) == 0)
    def _():
        for g in range(owners):
            right[:, g * depth : (g + 1) * depth] = r_ref[g, :, :, 0:res].reshape(depth, res).T

    many = max(16 // local, 1)
    for first in range(0, rows, 2):
        pair = min(2, rows - first)
        both = l_ref[first : first + pair].reshape(pair * seqs, outer)
        for d in range(0, inner, many):
            made = [dot(both, w_ref[:, (d + m) * cz : (d + m + 1) * cz]) for m in range(many)]
            for n in range(pair):
                for g in range(owners):
                    at = n * seqs + g * local
                    lines = jnp.concatenate([t[at : at + local] for t in made], axis=0).astype(BF16)
                    to = g * depth + d * local
                    mix[to : to + many * local, n * cz : (n + 1) * cz] = lines
        total = dot(right[...], mix[:, 0 : pair * cz])
        for n in range(pair):
            mine = jnp.broadcast_to(vi_ref[:, first + n : first + n + 1], (seqs, cz)).astype(BF16)
            tally = jnp.maximum(dot(vt_ref[...], mine), 1.0)
            o_ref[first + n] = total[:, n * cz : (n + 1) * cz] / tally


def opm_block(left, right, w, valid_t, mine):
    owned, seqs, outer = left.shape
    _, inner, _, _ = right.shape
    res = valid_t.shape[0]
    cz = w.shape[1] // inner
    rows = divisor(owned, 8)
    pair = pl.BlockSpec((rows, res, cz), lambda g: (g, 0, 0))
    return pl.pallas_call(
        opm_kernel,
        grid=(owned // rows,),
        in_specs=[
            pl.BlockSpec((rows, seqs, outer), lambda g: (g, 0, 0)),
            full(right.shape),
            full(w.shape),
            full(valid_t.shape),
            pl.BlockSpec((None, seqs, rows), lambda g: (g, 0, 0)),
        ],
        out_specs=pair,
        out_shape=jax.ShapeDtypeStruct((owned, res, cz), F32),
        scratch_shapes=[pltpu.VMEM((seqs * inner, 2 * cz), BF16), pltpu.VMEM((res, seqs * inner), BF16)],
        name="opm_block",
    )(left, right, w, valid_t, mine.reshape(seqs, owned // rows, rows).transpose(1, 0, 2))


def tail_kernel(table_ref, x_ref, tri_ref, opm_ref, wg_ref, wt_ref, w1_ref, w2_ref, *refs):
    o_ref, scr = refs[-2:]
    rows, groups, lines, cz = x_ref.shape
    cols = groups * lines
    many = divisor(rows, TAIL_ROWS)
    for n in range(scr.shape[0]):
        part = tri_ref[:, :, n * LANES : (n + 1) * LANES]
        scr[n] = part.astype(F32).reshape(scr.shape[1:])

    def block(b, carry):
        i = b * many
        x = x_ref[pl.ds(i, many)].reshape(many * cols, cz).astype(F32)
        gate = jax.nn.sigmoid(dot(norm(x).astype(BF16), wg_ref[...]))
        tri = [dot(norm(get_rows(scr, i + m, rows), 0).astype(BF16), wt_ref[...], 0, 0) for m in range(many)]
        one = x + gate * jnp.concatenate(tri, axis=0)
        hidden = jnp.maximum(dot(norm(one).astype(BF16), w1_ref[...]), 0.0).astype(BF16)
        out = one + dot(hidden, w2_ref[...]) + opm_ref[pl.ds(i, many)].reshape(many * cols, cz)
        o_ref[pl.ds(i, many)] = out.astype(o_ref.dtype).reshape(many, groups, lines, cz)
        return carry

    lax.fori_loop(0, rows // many, block, 0, unroll=TAIL_UNROLL)


def pair_tail(table, parts, x, tri, opm, weights, earlier=None):
    owned, res, cz = x.shape
    ring = res // owned
    rows = divisor(owned, 16)
    lines = owned // parts
    span = ring // 2 * lines
    view = (owned, ring, parts, lines, cz)
    pair = pl.BlockSpec((rows, ring // 2, None, lines, cz), lambda q, g, t: (g, t[0, q], t[1, q], 0, 0))
    in_specs = [pair, pl.BlockSpec((cz, rows, span), lambda q, g, t: (0, g, q)), pair]
    in_specs += [full(w.shape) for w in weights]
    args = [table, x.reshape(view), tri, opm.reshape(view), *weights]
    aliases = {}
    if earlier is not None:
        aliases = {len(args): 0}
        in_specs.append(pl.BlockSpec(memory_space=pl.ANY))
        args.append(earlier.reshape(view))
    return pl.pallas_call(
        tail_kernel,
        grid_spec=pltpu.PrefetchScalarGridSpec(
            num_scalar_prefetch=1,
            grid=(tri.shape[2] // span, owned // rows),
            in_specs=in_specs,
            out_specs=pair,
            scratch_shapes=[pltpu.VMEM((max(span // LANES, 1), cz * rows, min(span, LANES)), F32)],
        ),
        out_shape=jax.ShapeDtypeStruct(view, BF16),
        input_output_aliases=aliases,
        name="pair_tail",
    )(*args).reshape(owned, res, cz)


def body(
    ring,
    coupling_features,
    aligned_features,
    aligned_entry_flags,
    amino_real_flags,
    coupling_offset_matrix,
    lookup_matrices,
    aligned_final_matrix,
    product_factor_matrices,
    product_final_matrix,
    trio_factor_matrices,
    trio_final_matrix,
    feedforward_expand,
    feedforward_shrink,
):
    owned, res, cz = coupling_features.shape
    seqs, _, feat = aligned_features.shape
    width = feat // coupling_offset_matrix.shape[1]
    outer = product_factor_matrices.shape[1] // 2
    place = lax.axis_index("row")
    near = ring // 2
    halves = [list(range(near)), list(range(near, ring))]
    swap = [(r, (r + near) % ring) for r in range(ring)]

    residue = amino_real_flags.astype(F32)
    entry = aligned_entry_flags.astype(F32) * residue[None, :]
    my_residue = lax.dynamic_slice_in_dim(residue, place * owned, owned, 0)
    my_entry = lax.dynamic_slice_in_dim(entry, place * seqs, seqs, 0)
    trio = trio_factor_matrices.T

    parts = 2 if owned % 32 == 0 else 1
    half = (place // near).astype(jnp.int32)

    def spread(values):
        values = values.reshape(near, cz // near, values.shape[1], values.shape[-1])
        return lax.all_to_all(values, "row", 0, 0, tiled=True, axis_index_groups=halves)

    bias = pair_bias(coupling_features, coupling_offset_matrix.T)
    made = []
    for part in range(parts):
        made.append(
            pair_head(coupling_features, my_residue, residue, trio[2 * cz : 4 * cz], part, parts)
        )

    planes = 4 if ring % 4 == 0 else 1
    members = ring // planes
    plane = place // members
    within = [[m + members * z for m in range(members)] for z in range(planes)]
    order = [m * planes + z for z in range(planes) for m in range(members)]

    def across(values):
        got = [values[0]]
        for k in range(1, planes):
            got.append(lax.ppermute(values[k], "row", [(r, r ^ (k * members)) for r in range(ring)]))
        got = jnp.stack(got)
        return jnp.stack([lax.dynamic_index_in_dim(got, plane ^ z, 0, keepdims=False) for z in range(planes)])

    def gather(values):
        values = lax.all_gather(values, "row", axis=0, axis_index_groups=within)
        return values.reshape((ring,) + values.shape[2:])

    bias = across([bias] * planes)
    right_own, right_oth = [], []
    for part in range(parts):
        right = made[part]
        if part:
            right, bias = lax.optimization_barrier((right, bias))
        right_own.append(spread(right))
        right_oth.append(lax.ppermute(right_own[part], "row", swap))
    left = pair_head(coupling_features, my_residue, residue, trio[0 : 2 * cz])
    left_own = spread(left)
    bias_all = gather(bias)

    msa_out, left_opm, right_opm = msa_block(
        aligned_features,
        my_entry,
        bias_all,
        order,
        lookup_matrices,
        aligned_final_matrix,
        product_factor_matrices.T,
        width,
    )

    def collect(sums):
        back = lax.all_to_all(sums, "row", 0, 0, tiled=True, axis_index_groups=halves)
        return back.reshape(cz, owned, sums.shape[-1])

    spot = res // planes
    both = []
    for k in range(planes):
        lines = lax.dynamic_slice_in_dim(left_opm, (plane ^ k) * spot, spot, 2)
        both.append(jnp.concatenate([right_opm, lines], axis=2).transpose(1, 0, 2))
    both = gather(across(both))
    left_res = lax.dynamic_slice_in_dim(both, res + (place % members) * owned, owned, 3)
    left_res = left_res.transpose(3, 0, 2, 1).reshape(owned, ring * seqs, outer)
    entry_order = entry.reshape(planes, members, seqs, res).transpose(1, 0, 2, 3).reshape(ring * seqs, res)
    mine = lax.dynamic_slice_in_dim(entry_order, place * owned, owned, 1)
    outer_map = product_final_matrix.reshape(outer, outer * cz)
    gate_map = trio_factor_matrices[:, 4 * cz : 5 * cz]
    entry_t = entry_order.T.astype(BF16)
    left_own, left_res, outer_map, gate_map, entry_t, mine = lax.optimization_barrier(
        (left_own, left_res, outer_map, gate_map, entry_t, mine)
    )
    opm = opm_block(left_res, both, outer_map, entry_t, mine)

    sums = tri_sums(left_own, right_own + right_oth[:-1])
    tri_near = collect(sums)
    sums = tri_sums(left_own, right_oth[-1:])
    tri_last = collect(sums)
    weights = (gate_map, trio_final_matrix, feedforward_expand, feedforward_shrink)
    table = jnp.array([[0] * parts + [1] * parts, list(range(parts)) * 2], jnp.int32)
    table = table.at[0].set(table[0] ^ half)
    pair = pair_tail(table[:, :-1], parts, coupling_features, tri_near, opm, weights)
    pair = pair_tail(table[:, -1:], parts, coupling_features, tri_last, opm, weights, earlier=pair)
    return (msa_out, pair)


def solution(mesh):


    return jax.shard_map(
        functools.partial(body, mesh.shape["row"]),
        mesh=mesh,
        in_specs=(
            P(("grp", "row"), None, None),
            P(("grp", "row"), None, None),
            P("grp", None),
            P("grp"),
            P(),
            P(),
            P(),
            P(),
            P(),
            P(),
            P(),
            P(),
            P(),
        ),
        out_specs=(P(("grp", "row"), None, None), P(("grp", "row"), None, None)),
        check_vma=False,
    )
```
